32 devices in a mesh: fsdp: 4 (over y, x), seq: 8 (over z, core).
Axes of the slice: x: 2, y: 2, z: 4, core: 2. Of those that a mesh axis runs over, the one named last changes fastest.
Arguments:
- inputs: bfloat16 [4, 2048, 2048], P('fsdp', 'seq'), may hold values from -6 to 6
- documents: int32 [4, 2048], P('fsdp'), may hold values from 0 to 3, never falling along the last dimension, each value on 1 to 1024 neighbouring positions
- cotangent: bfloat16 [4, 2048, 2048], P('fsdp', 'seq'), may hold values from -6 to 6
- attend_gain: bfloat16 [2048], P('fsdp'), may hold values from 0.5 to 1.5
- attend_shift: bfloat16 [2048], P('fsdp'), may hold values from -2 to 2
- project_in: bfloat16 [2048, 6144], P('fsdp'), may hold values from -0.125 to 0.125
- project_bias: bfloat16 [2, 2048], P(None, 'fsdp'), may hold values from -2 to 2
- project_out: bfloat16 [2048, 2048], P('fsdp'), may hold values from -0.5 to 0.5
- output_bias: bfloat16 [2048], P('fsdp'), may hold values from -2 to 2
- feed_gain: bfloat16 [2048], P('fsdp'), may hold values from 0.5 to 1.5
- feed_shift: bfloat16 [2048], P('fsdp'), may hold values from -2 to 2
- expand_weight: bfloat16 [2048, 8192], P('fsdp'), may hold values from -0.125 to 0.125
- expand_bias: bfloat16 [8192], P('fsdp'), may hold values from -2 to 2
- reduce_weight: bfloat16 [8192, 2048], P('fsdp'), may hold values from -0.0625 to 0.0625
- reduce_bias: bfloat16 [2048], P('fsdp'), may hold values from -2 to 2
Outputs:
- layer_output: bfloat16 [4, 2048, 2048], P('fsdp', 'seq')
- input_gradient: float32 [4, 2048, 2048], P('fsdp', 'seq')
- attend_gain_gradient: float32 [2048], P('fsdp')
- attend_shift_gradient: float32 [2048], P('fsdp')
- project_in_gradient: float32 [2048, 6144], P('fsdp')
- project_bias_gradient: float32 [2, 2048], P(None, 'fsdp')
- project_out_gradient: float32 [2048, 2048], P('fsdp')
- output_bias_gradient: float32 [2048], P('fsdp')
- feed_gain_gradient: float32 [2048], P('fsdp')
- feed_shift_gradient: float32 [2048], P('fsdp')
- expand_weight_gradient: float32 [2048, 8192], P('fsdp')
- expand_bias_gradient: float32 [8192], P('fsdp')
- reduce_weight_gradient: float32 [8192, 2048], P('fsdp')
- reduce_bias_gradient: float32 [2048], P('fsdp')
The draws below stay inside these ranges and needn't reach their ends.
Inputs may be any that keep to these rules, and one draw needn't show every extreme that they name: `documents`: in each sequence the document numbers never fall, all 4 of them occur, each document has 1 to 1024 positions, and one has exactly 1024.
All inputs are finite; a program needn't handle non-finite values.
Results may differ from the reference program's by a relative error of at most 0.019.
Values may be sent and summed in bfloat16 or wider, within the bound.
No kernel may reach another device: no remote copies, remote signals or barrier semaphores. Data moves between devices by JAX's collectives and lax.ppermute only.
A program may use at most 512 MiB of HBM per device.

```python
import math
import jax
import jax.numpy as jnp
import numpy as np
from jax import lax

D = 2048
HEADS = 32
HEAD_DIM = 64
FF = 8192
BLOCK = 128
DOCS = 4
LENGTH = 2048
SEQS = 4
TOKENS = 8192


def steps_of(stream_key, shape, cuts, least, high):
    factor_of, own = 1.0, jax.random.fold_in(stream_key, 6)
    for dim, shards_of in cuts:
        steps = jnp.exp(jax.random.uniform(jax.random.fold_in(own, dim), (shards_of,), jnp.float32, least / len(cuts), high / len(cuts)))
        factor_of = factor_of * jnp.repeat(steps, shape[dim] // shards_of).reshape([-1 if axis == dim else 1 for axis in range(len(shape))])
    return factor_of


def length_profile(number_of, total, limit, skew):
    portions = [(1 << 20) // math.isqrt(rank ** skew) + 1 for rank in range(2, number_of + 1)]
    spare, counts = total - limit - (number_of - 1), [1] * (number_of - 1)
    while spare > 0:
        movable = [i for i in range(number_of - 1) if counts[i] < limit]
        whole, left = sum([portions[i] for i in movable]), spare
        for i in movable:
            more = min(limit - counts[i], max(1, left * portions[i] // whole), spare)
            counts[i] = counts[i] + more
            spare = spare - more
    return np.array([limit] + counts)


def ragged_sizes(rng, count, total, limit, slope):
    if count == 2:
        one = jax.random.randint(rng, (), max(1, total - limit), min(limit, total - 1) + 1)
        return jnp.stack([one, total - one])
    tallies = jnp.asarray(length_profile(count, total, limit, slope), jnp.int32)
    couples = (count - 1) // 2
    donor, taker = tallies[1:1 + 2 * couples:2], tallies[2:2 + 2 * couples:2]
    room = jnp.minimum(donor - 1, limit - taker)
    moved = jax.random.randint(jax.random.fold_in(rng, 1), (couples,), 0, 1 << 20) % (room + 1)
    tallies = tallies.at[1:1 + 2 * couples:2].set(donor - moved).at[2:2 + 2 * couples:2].set(taker + moved)
    return tallies[jax.random.permutation(jax.random.fold_in(rng, 2), count)]


def scatter_about(rng, dims, deviation, limit, cuts=(), held_as=jnp.bfloat16):
    gain = steps_of(rng, dims, cuts, -0.22, 0.18) if cuts else 1.0
    array = jax.random.normal(rng, dims, jnp.float32) * deviation * gain
    return jnp.minimum(jnp.maximum(array, -limit), limit).astype(held_as)


def setup_inputs(seed: int = 0) -> dict:
    splits = jax.random.split(jax.random.key(seed), 16)
    inputs = scatter_about(splits[0], (SEQS, LENGTH, D), 1.0, 6.0, ((0, 4), (1, 8)))
    documents = jax.vmap(lambda own: jnp.searchsorted(jnp.cumsum(ragged_sizes(own, DOCS, LENGTH, LENGTH // 2, 0)), jnp.arange(LENGTH), side="right"))(jax.random.split(splits[1], SEQS)).reshape((SEQS, LENGTH)).astype(jnp.int32)
    cotangent = scatter_about(splits[2], (SEQS, LENGTH, D), 1.0, 6.0, ((0, 4), (1, 8)))
    attend_gain = jnp.clip(1.0 + 0.1 * jax.random.normal(splits[3], (D,), jnp.float32), 0.5, 1.5).astype(jnp.bfloat16)
    attend_shift = scatter_about(splits[4], (D,), 0.3, 2.0, ((0, 4),))
    project_in = scatter_about(splits[5], (D, 3 * D), D ** -0.5, 0.125, ((0, 4),))
    project_bias = scatter_about(splits[6], (2, D), 0.3, 2.0, ((1, 4),))
    project_out = scatter_about(splits[7], (D, D), (D // 16) ** -0.5, 0.5, ((0, 4),))
    output_bias = scatter_about(splits[8], (D,), 0.3, 2.0, ((0, 4),))
    feed_gain = jnp.clip(1.0 + 0.1 * jax.random.normal(splits[9], (D,), jnp.float32), 0.5, 1.5).astype(jnp.bfloat16)
    feed_shift = scatter_about(splits[10], (D,), 0.3, 2.0, ((0, 4),))
    expand_weight = scatter_about(splits[11], (D, FF), D ** -0.5, 0.125, ((0, 4),))
    expand_bias = scatter_about(splits[12], (FF,), 0.3, 2.0, ((0, 4),))
    reduce_weight = scatter_about(splits[13], (FF, D), FF ** -0.5, 0.0625, ((0, 4),))
    reduce_bias = scatter_about(splits[14], (D,), 0.3, 2.0, ((0, 4),))
    return {"inputs": inputs, "documents": documents, "cotangent": cotangent, "attend_gain": attend_gain, "attend_shift": attend_shift, "project_in": project_in, "project_bias": project_bias, "project_out": project_out, "output_bias": output_bias, "feed_gain": feed_gain, "feed_shift": feed_shift, "expand_weight": expand_weight, "expand_bias": expand_bias, "reduce_weight": reduce_weight, "reduce_bias": reduce_bias}


@jax.custom_vjp
def low(v):
    return lax.optimization_barrier(v.astype(jnp.bfloat16)).astype(jnp.float32)

@jax.custom_vjp
def low_back(v):
    return v

def low_keep(v):
    return (low(v), None)

def low_pass(kept, grad):
    return (grad,)

def back_keep(v):
    return (v, None)

def back_low(kept, grad):
    return (low(grad),)
low.defvjp(low_keep, low_pass)
low_back.defvjp(back_keep, back_low)
epsilon = 1e-05
highest = lax.Precision.HIGHEST

def layer_norm(values, gain_vector, shift_vector):
    centre = lax.optimization_barrier(jnp.mean(values, axis=-1, keepdims=True))
    offset = values - centre
    spread = lax.optimization_barrier(jnp.mean(offset * offset, axis=-1, keepdims=True))
    return offset * lax.rsqrt(spread + epsilon) * gain_vector + shift_vector

def product(former, latter):
    return jnp.dot(former, latter, precision=highest, preferred_element_type=jnp.float32)

def sequence_layer(token_rows, doc_row, params):
    attend_gain, attend_shift, project_in, project_bias, project_out, output_bias, feed_gain, feed_shift, expand_weight, expand_bias, reduce_weight, reduce_bias = params
    seq_length = token_rows.shape[0]
    normed_first = low(layer_norm(token_rows, attend_gain, attend_shift))
    zero_bias = jnp.zeros_like(project_bias[0])
    full_bias = jnp.concatenate([project_bias[0], zero_bias, project_bias[1]])
    projected = low_back(low(product(normed_first, project_in) + full_bias))
    split_heads = projected.reshape(seq_length, 3, HEADS, HEAD_DIM)
    queries = split_heads[:, 0]
    keys_all = split_heads[:, 1]
    values_all = split_heads[:, 2]
    slopes = 2.0 ** (-8.0 * (jnp.arange(HEADS) + 1).astype(jnp.float32) / HEADS)
    positions = jnp.arange(seq_length, dtype=jnp.int32)
    row_block = min(512, seq_length)

    def attend_block(start):
        query_block = lax.dynamic_slice_in_dim(queries, start, row_block)
        logits = jnp.einsum('qhd,khd->hqk', query_block, keys_all, precision=highest) * HEAD_DIM ** (-0.5)
        query_pos = start + jnp.arange(row_block, dtype=jnp.int32)
        distance = jnp.abs(query_pos[:, None] - positions[None, :]).astype(jnp.float32)
        logits = logits - slopes[:, None, None] * distance[None]
        query_docs = lax.dynamic_slice_in_dim(doc_row, start, row_block)
        allowed = (query_docs[:, None] == doc_row[None, :]) & (positions[None, :] // BLOCK <= query_pos[:, None] // BLOCK)
        logits = low_back(jnp.where(allowed[None], logits, -jnp.inf))
        row_peak = lax.optimization_barrier(jnp.max(logits, axis=-1, keepdims=True))
        weights_exp = jnp.exp(logits - row_peak)
        probs = low(weights_exp / lax.optimization_barrier(jnp.sum(weights_exp, axis=-1, keepdims=True)))
        return jnp.einsum('hqk,khd->qhd', probs, values_all, precision=highest)
    starts = jnp.arange(seq_length // row_block, dtype=jnp.int32) * row_block
    attended = lax.map(jax.checkpoint(attend_block), starts).reshape(seq_length, HEADS * HEAD_DIM)
    attended = low_back(low(attended))
    middle = token_rows + low_back(product(attended, project_out) + output_bias)
    normed_second = low(layer_norm(middle, feed_gain, feed_shift))
    hidden_pre = low_back(product(normed_second, expand_weight) + expand_bias)
    activated = low(jax.nn.gelu(hidden_pre, approximate=False))
    return middle + product(activated, reduce_weight) + reduce_bias

def reference(inputs, documents, cotangent, attend_gain, attend_shift, project_in, project_bias, project_out, output_bias, feed_gain, feed_shift, expand_weight, expand_bias, reduce_weight, reduce_bias):
    weights = (attend_gain.astype(jnp.float32), attend_shift.astype(jnp.float32), project_in.astype(jnp.float32), project_bias.astype(jnp.float32), project_out.astype(jnp.float32), output_bias.astype(jnp.float32), feed_gain.astype(jnp.float32), feed_shift.astype(jnp.float32), expand_weight.astype(jnp.float32), expand_bias.astype(jnp.float32), reduce_weight.astype(jnp.float32), reduce_bias.astype(jnp.float32))

    def one_sequence(carry, pieces):
        token_rows, doc_row, grad_rows = pieces
        layer_out, back_fn = jax.vjp(lambda rows_in, params: sequence_layer(rows_in, doc_row, params), token_rows.astype(jnp.float32), weights)
        grad_in, grad_params = back_fn(grad_rows.astype(jnp.float32))
        carry = jax.tree.map(lambda running_sum, new_term: running_sum + new_term, carry, grad_params)
        return (carry, (layer_out.astype(jnp.bfloat16), grad_in))
    initial = jax.tree.map(jnp.zeros_like, weights)
    totals, (layer_output, input_gradient) = lax.scan(one_sequence, initial, (inputs, documents, cotangent))
    factor = TOKENS ** (-0.5)
    return (layer_output, input_gradient, totals[0] * factor, totals[1] * factor, totals[2] * factor, totals[3] * factor, totals[4] * factor, totals[5] * factor, totals[6] * factor, totals[7] * factor, totals[8] * factor, totals[9] * factor, totals[10] * factor, totals[11] * factor)
```

```python
import functools

import jax
import jax.numpy as jnp
from jax import lax
from jax.experimental import pallas as pl
from jax.experimental.pallas import tpu as pltpu
from jax.sharding import Mesh, PartitionSpec as P

HEADS = 32
HEAD_DIM = 64
BLOCK = 128
DOCS = 4
TILE = 256
CORES = 2
MASKED = -1e30

epsilon = 1e-05
bf16 = jnp.bfloat16
f32 = jnp.float32


def contract(a, b, da, db):
    return lax.dot_general(a, b, (((da,), (db,)), ((), ())), preferred_element_type=f32)


def tile_bias(bias_ref, slope_ref, pair):
    keys = lax.broadcasted_iota(jnp.int32, (TILE, TILE), 0)
    queries = lax.broadcasted_iota(jnp.int32, (TILE, TILE), 1)
    gap = (keys - queries).astype(f32)
    for h in range(2):
        bias_ref[h] = gap * slope_ref[pair * 2 + h]


def head_halves(block):
    lane = lax.broadcasted_iota(jnp.int32, block.shape, 1)
    zero = jnp.zeros_like(block)
    return [jnp.where((lane // HEAD_DIM) == h, block, zero) for h in range(2)]


def forward_kernel(
    first_ref, slope_ref, q_ref, k_ref, v_ref, low_ref, high_ref, out_ref, lse_ref, vt_ref, bias_ref
):
    pair, qi = pl.program_id(0), pl.program_id(1)

    @pl.when(qi == 0)
    def _():
        vt_ref[...] = v_ref[...].T
        tile_bias(bias_ref, slope_ref, pair)

    queries = head_halves(q_ref[...] * jnp.asarray(HEAD_DIM**-0.5, bf16))
    low, high = low_ref[...], high_ref[...]
    rows = lax.broadcasted_iota(jnp.int32, (TILE, TILE), 0)
    here = pl.multiple_of(qi * TILE, TILE)
    diagonal = k_ref[pl.ds(here, TILE), :]
    inside = (rows >= low - here) & (rows < high - here)
    state = []
    for h in range(2):
        scores = contract(diagonal, queries[h], 1, 1) - jnp.abs(bias_ref[h])
        scores = jnp.where(inside, scores, MASKED)
        peak = jnp.max(scores, axis=0, keepdims=True)
        weights = jnp.exp(scores - peak)
        total = jnp.sum(weights, axis=0, keepdims=True)
        values = vt_ref[pl.ds(h * HEAD_DIM, HEAD_DIM), pl.ds(here, TILE)]
        state += [peak, total, contract(values, weights.astype(bf16), 1, 0)]

    def step(t, state):
        start = pl.multiple_of(t * TILE, TILE)
        keys = k_ref[pl.ds(start, TILE), :]
        seen = rows >= low - start
        away = ((t - qi) * TILE).astype(f32)
        fresh = []
        for h in range(2):
            peak, total, mixed = state[3 * h : 3 * h + 3]
            scores = contract(keys, queries[h], 1, 1) + bias_ref[h]
            scores = jnp.where(seen, scores, MASKED)
            offset = away * slope_ref[pair * 2 + h]
            top = jnp.maximum(peak, jnp.max(scores, axis=0, keepdims=True) + offset)
            weights = jnp.exp(scores + (offset - top))
            shrink = jnp.exp(peak - top)
            values = vt_ref[pl.ds(h * HEAD_DIM, HEAD_DIM), pl.ds(start, TILE)]
            fresh += [
                top,
                total * shrink + jnp.sum(weights, axis=0, keepdims=True),
                mixed * shrink + contract(values, weights.astype(bf16), 1, 0),
            ]
        return tuple(fresh)

    state = lax.fori_loop(first_ref[qi], qi, step, tuple(state))
    mixed = jnp.concatenate([state[2] / state[1], state[5] / state[4]], axis=0)
    out_ref[...] = mixed.T.astype(bf16)
    lse_ref[0] = jnp.concatenate([state[0] + jnp.log(state[1]), state[3] + jnp.log(state[4])], axis=0)


def backward_kernel(
    first_ref,
    slope_ref,
    q_ref,
    k_ref,
    v_ref,
    out_ref,
    grad_ref,
    lse_ref,
    low_ref,
    high_ref,
    dq_ref,
    dk_ref,
    dv_ref,
    kt_ref,
    bias_ref,
    dk_sum,
    dv_sum,
    dq_sum,
):
    pair, qi = pl.program_id(0), pl.program_id(1)

    @pl.when(qi == 0)
    def _():
        kt_ref[...] = k_ref[...].T
        tile_bias(bias_ref, slope_ref, pair)
        dk_sum[...] = jnp.zeros_like(dk_sum)
        dv_sum[...] = jnp.zeros_like(dv_sum)

    queries = head_halves(q_ref[...] * jnp.asarray(HEAD_DIM**-0.5, bf16))
    grads = head_halves(grad_ref[...])
    low, high = low_ref[...], high_ref[...]
    rows = lax.broadcasted_iota(jnp.int32, (TILE, TILE), 0)
    product = (grad_ref[...].astype(f32) * out_ref[...].astype(f32)).T
    deltas = [
        jnp.sum(product[h * HEAD_DIM : (h + 1) * HEAD_DIM], axis=0, keepdims=True) for h in range(2)
    ]
    lse = [lse_ref[0, pl.ds(h, 1), :] for h in range(2)]
    dq_sum[...] = jnp.zeros_like(dq_sum)

    def tile(start, on_diagonal, offsets):
        keys = k_ref[pl.ds(start, TILE), :]
        values = v_ref[pl.ds(start, TILE), :]
        seen = rows >= low - start
        if on_diagonal:
            seen = seen & (rows < high - start)
        dk, dv = dk_sum[pl.ds(start, TILE), :], dv_sum[pl.ds(start, TILE), :]
        for h in range(2):
            scores = contract(keys, queries[h], 1, 1)
            if on_diagonal:
                scores = scores - jnp.abs(bias_ref[h]) - lse[h]
            else:
                scores = scores + bias_ref[h] + (offsets[h] - lse[h])
            probs = jnp.exp(jnp.where(seen, scores, MASKED))
            pull = contract(values, grads[h], 1, 1)
            grad_scores = (probs * (pull - deltas[h])).astype(bf16)
            dv = dv + contract(probs.astype(bf16), grads[h], 1, 0)
            dk = dk + contract(grad_scores, queries[h], 1, 0)
            keys_t = kt_ref[pl.ds(h * HEAD_DIM, HEAD_DIM), pl.ds(start, TILE)]
            dq_sum[pl.ds(h * HEAD_DIM, HEAD_DIM), :] += contract(keys_t, grad_scores, 1, 0)
        dk_sum[pl.ds(start, TILE), :] = dk
        dv_sum[pl.ds(start, TILE), :] = dv

    tile(pl.multiple_of(qi * TILE, TILE), True, None)

    def step(t, carry):
        away = ((t - qi) * TILE).astype(f32)
        tile(
            pl.multiple_of(t * TILE, TILE),
            False,
            [away * slope_ref[pair * 2 + h] for h in range(2)],
        )
        return carry

    lax.fori_loop(first_ref[qi], qi, step, 0)
    dq_ref[...] = (dq_sum[...] * HEAD_DIM**-0.5).T.astype(bf16)

    @pl.when(qi == pl.num_programs(1) - 1)
    def _():
        dk_ref[...] = dk_sum[...].astype(bf16)
        dv_ref[...] = dv_sum[...].astype(bf16)


def attention_specs(length, pairs):
    wide = 2 * HEAD_DIM

    def tiles(third):
        return pl.BlockSpec((TILE, wide), lambda p, i, *_: (i, third * pairs + p))

    def whole(third):
        return pl.BlockSpec((length, wide), lambda p, i, *_: (0, third * pairs + p))

    limits = pl.BlockSpec((1, TILE), lambda p, i, *_: (0, i))
    lse = pl.BlockSpec((1, 2, TILE), lambda p, i, *_: (p, 0, i))
    return tiles, whole, limits, lse


def attention(stacked, low, high, first, slopes):
    length, pairs = stacked.shape[0], stacked.shape[1] // (6 * HEAD_DIM)
    tiles, whole, limits, lse = attention_specs(length, pairs)
    return pl.pallas_call(
        forward_kernel,
        grid_spec=pltpu.PrefetchScalarGridSpec(
            num_scalar_prefetch=2,
            grid=(pairs, length // TILE),
            in_specs=[tiles(0), whole(1), whole(2), limits, limits],
            out_specs=[tiles(0), lse],
            scratch_shapes=[
                pltpu.VMEM((2 * HEAD_DIM, length), bf16),
                pltpu.VMEM((2, TILE, TILE), f32),
            ],
        ),
        out_shape=[
            jax.ShapeDtypeStruct((length, pairs * 2 * HEAD_DIM), bf16),
            jax.ShapeDtypeStruct((pairs, 2, length), f32),
        ],
        compiler_params=pltpu.CompilerParams(vmem_limit_bytes=32 << 20),
        cost_estimate=pl.CostEstimate(
            flops=16_000_000_000, bytes_accessed=8 << 20, transcendentals=8 << 20
        ),
        name="attention_forward",
    )(first, slopes, stacked, stacked, stacked, low, high)


def attention_back(stacked, mixed, grads, lse_rows, low, high, first, slopes):
    length, pairs = stacked.shape[0], stacked.shape[1] // (6 * HEAD_DIM)
    tiles, whole, limits, lse = attention_specs(length, pairs)
    shape = jax.ShapeDtypeStruct((length, pairs * 2 * HEAD_DIM), bf16)
    return pl.pallas_call(
        backward_kernel,
        grid_spec=pltpu.PrefetchScalarGridSpec(
            num_scalar_prefetch=2,
            grid=(pairs, length // TILE),
            in_specs=[tiles(0), whole(1), whole(2), tiles(0), tiles(0), lse, limits, limits],
            out_specs=[tiles(0), whole(0), whole(0)],
            scratch_shapes=[
                pltpu.VMEM((2 * HEAD_DIM, length), bf16),
                pltpu.VMEM((2, TILE, TILE), f32),
                pltpu.VMEM((length, 2 * HEAD_DIM), f32),
                pltpu.VMEM((length, 2 * HEAD_DIM), f32),
                pltpu.VMEM((2 * HEAD_DIM, TILE), f32),
            ],
        ),
        out_shape=[shape, shape, shape],
        compiler_params=pltpu.CompilerParams(vmem_limit_bytes=32 << 20),
        cost_estimate=pl.CostEstimate(
            flops=40_000_000_000, bytes_accessed=16 << 20, transcendentals=8 << 20
        ),
        name="attention_backward",
    )(first, slopes, stacked, stacked, stacked, mixed, grads, lse_rows, low, high)


def moments(values):
    centre = jnp.mean(values, axis=-1, keepdims=True)
    offset = values - centre
    rate = lax.rsqrt(jnp.mean(offset * offset, axis=-1, keepdims=True) + epsilon)
    return offset * rate, rate


def norm_back(grads, unit, rate, gain):
    scaled = grads * gain
    mean = jnp.mean(scaled, axis=-1, keepdims=True)
    along = jnp.mean(scaled * unit, axis=-1, keepdims=True)
    return rate * (scaled - mean - unit * along)


def dot(a, b):
    return jnp.dot(a, b, preferred_element_type=f32)


def gelu_parts(values):
    phi = 0.5 * (1.0 + lax.erf(values * (0.5**0.5)))
    density = jnp.exp(-0.5 * values * values) * 0.3989422804014327
    return values * phi, phi + values * density


def swap_cores(values):
    return lax.ppermute(values, "c", [(0, 1), (1, 0)])


def plane_gather(rows):
    n = lax.axis_size("f")
    spread = jnp.broadcast_to(rows[None], (n,) + rows.shape)
    mine = lax.all_to_all(spread, "f", split_axis=0, concat_axis=0, tiled=True)
    return jnp.stack([mine, swap_cores(mine)])


def plane_scatter(partial):
    near = partial[0].astype(f32) + swap_cores(partial[1]).astype(f32)
    parts = lax.all_to_all(near.astype(bf16), "f", split_axis=0, concat_axis=0, tiled=True)
    return jnp.sum(parts.astype(f32), axis=0)


def local(
    inputs,
    documents,
    cotangent,
    attend_gain,
    attend_shift,
    project_in,
    project_bias,
    project_out,
    output_bias,
    feed_gain,
    feed_shift,
    expand_weight,
    expand_bias,
    reduce_weight,
    reduce_bias,
):
    columns, planes = lax.axis_size("f"), lax.axis_size("z")
    me_f, me_c = lax.axis_index("f"), lax.axis_index("c")
    owned, width = inputs.shape[1], inputs.shape[2]
    length = documents.shape[1]
    hidden = expand_weight.shape[1]
    device_heads = HEADS // (columns * CORES)
    group = device_heads * HEAD_DIM
    ff = hidden // (columns * CORES)
    scaling = (columns * length) ** (-0.5)

    turn = [(a * planes + b, b * planes + a) for a in range(columns) for b in range(planes)]

    def transpose_planes(values):
        return lax.ppermute(values, ("f", "z"), turn)

    def own_core(values, axis):
        return lax.dynamic_index_in_dim(values, me_c, axis, keepdims=False)

    tokens = transpose_planes(inputs[0])
    docs = transpose_planes(documents)
    grad_own = transpose_planes(cotangent[0])

    vectors = jnp.stack([attend_gain, attend_shift, output_bias, feed_gain, feed_shift, reduce_bias])
    vectors = lax.all_gather(vectors, "f", axis=1, tiled=True).astype(f32)
    gain_one, shift_one, bias_out, gain_two, shift_two, bias_reduce = vectors

    thirds = own_core(project_in.reshape(-1, 3, columns, CORES, group), 3)
    weight_in = lax.all_to_all(thirds, "f", split_axis=2, concat_axis=0, tiled=True)
    weight_in = weight_in.reshape(width, 3 * group)
    slices = own_core(expand_weight.reshape(-1, columns, CORES, ff), 2)
    weight_up = lax.all_to_all(slices, "f", split_axis=1, concat_axis=0, tiled=True)
    weight_up = weight_up.reshape(width, ff)
    weight_out = own_core(project_out.reshape(CORES, group, width), 0)
    weight_down = own_core(reduce_weight.reshape(CORES, ff, width), 0)
    bias_pair = own_core(project_bias.reshape(2, CORES, group), 1).astype(f32)
    bias_in = jnp.concatenate([bias_pair[0], jnp.zeros((group,), f32), bias_pair[1]])
    bias_up = own_core(expand_bias.reshape(CORES, ff), 0).astype(f32)

    doc_row = docs[0]
    position = jnp.arange(length, dtype=jnp.int32)
    low = jnp.zeros_like(doc_row)
    end = jnp.zeros_like(doc_row)
    for d in range(DOCS):
        low = jnp.where(doc_row == d, jnp.sum((doc_row < d).astype(jnp.int32)), low)
        end = jnp.where(doc_row == d, jnp.sum((doc_row <= d).astype(jnp.int32)), end)
    high = jnp.minimum(end, (position // BLOCK + 1) * BLOCK)
    first = low[::TILE] // TILE
    low, high = low[None], high[None]
    first_head = (me_f * CORES + me_c) * device_heads
    heads = first_head + 1 + jnp.arange(device_heads, dtype=jnp.int32)
    slopes = 2.0 ** (-8.0 * heads.astype(f32) / HEADS)

    def natural(values):
        cores = [lax.dynamic_index_in_dim(values, me_c ^ k, 0, keepdims=False) for k in range(CORES)]
        return jnp.stack(cores, axis=1).reshape(length, values.shape[-1])

    def relative(values):
        split = values.reshape(columns, CORES, owned, values.shape[-1])
        cores = [lax.dynamic_index_in_dim(split, me_c ^ k, 1, keepdims=False) for k in range(CORES)]
        return jnp.stack(cores).reshape(length, values.shape[-1])

    def split_rows(values):
        return values.reshape(CORES, columns, owned, values.shape[-1])

    token_rows = tokens.astype(f32)
    unit_one, rate_one = moments(token_rows)
    normed_one = plane_gather((unit_one * gain_one + shift_one).astype(bf16)).reshape(length, width)
    projected = (dot(normed_one, weight_in) + bias_in).astype(bf16)
    stacked = natural(split_rows(projected))
    mixed, lse_rows = attention(stacked, low, high, first, slopes)
    mixed_rel = relative(mixed)
    branch = plane_scatter(split_rows(dot(mixed_rel, weight_out).astype(bf16)))
    middle = token_rows + (branch + bias_out)
    unit_two, rate_two = moments(middle)
    normed_two = plane_gather((unit_two * gain_two + shift_two).astype(bf16)).reshape(length, width)
    hidden_pre = dot(normed_two, weight_up) + bias_up
    active, slope = gelu_parts(hidden_pre)
    active = active.astype(bf16)

    grad_all = plane_gather(grad_own).reshape(length, width)
    grad_active = contract(grad_all, weight_down, 1, 1)
    grad_hidden = (grad_active * slope).astype(bf16)
    grad_two = plane_scatter(split_rows(contract(grad_hidden, weight_up, 1, 1).astype(bf16)))
    down_term = contract(active, grad_all, 0, 0).astype(bf16)
    up_term = contract(normed_two, grad_hidden, 0, 0).astype(bf16)
    down_share = lax.psum_scatter(down_term, "z", scatter_dimension=0, tiled=True)
    up_share = lax.psum_scatter(
        up_term.reshape(columns, -1, ff), "z", scatter_dimension=1, tiled=True
    )

    grad_rows = grad_own.astype(f32)
    grad_middle = grad_rows + norm_back(grad_two, unit_two, rate_two, gain_two)
    grad_branch = grad_middle.astype(bf16)
    branch_all = plane_gather(grad_branch).reshape(length, width)
    grad_mixed = natural(split_rows(contract(branch_all, weight_out, 1, 1).astype(bf16)))
    out_term = contract(mixed_rel, branch_all, 0, 0).astype(bf16)
    out_share = lax.psum_scatter(out_term, "z", scatter_dimension=0, tiled=True)

    forward_sum = plane_scatter(split_rows(dot(active, weight_down).astype(bf16)))
    layer_rows = (middle + forward_sum + bias_reduce).astype(bf16)
    layer_output = transpose_planes(layer_rows)

    dq, dk, dv = attention_back(stacked, mixed, grad_mixed, lse_rows, low, high, first, slopes)
    grad_projected = relative(jnp.concatenate([dq, dk, dv], axis=1))
    grad_one = plane_scatter(split_rows(contract(grad_projected, weight_in, 1, 1).astype(bf16)))
    in_term = contract(normed_one, grad_projected, 0, 0).astype(bf16)
    in_share = lax.psum_scatter(
        in_term.reshape(columns, -1, 3 * group), "z", scatter_dimension=1, tiled=True
    )
    input_rows = grad_middle + norm_back(grad_one, unit_one, rate_one, gain_one)
    input_gradient = transpose_planes(input_rows.astype(bf16)).astype(f32)

    def spread(share):
        return lax.all_gather(share, ("z", "c"), axis=0, tiled=False).reshape(
            (planes, CORES) + share.shape
        )

    def turned(share):
        return lax.all_to_all(share, "f", split_axis=0, concat_axis=0, tiled=True)

    def by_rows(share):
        full = spread(share).transpose(1, 0, 2, 3)
        return full.reshape(-1, width).astype(f32) * scaling

    down_gradient = by_rows(down_share)
    up_all = spread(turned(up_share))
    up_gradient = up_all.transpose(0, 3, 2, 1, 4).reshape(-1, hidden).astype(f32) * scaling
    out_gradient = by_rows(out_share)
    in_all = spread(turned(in_share))
    in_all = in_all.reshape(in_all.shape[:4] + (3, group))
    in_gradient = in_all.transpose(0, 3, 4, 2, 1, 5).reshape(-1, 3 * width).astype(f32) * scaling

    sums = jnp.stack(
        [
            jnp.sum(grad_one * unit_one, axis=0),
            jnp.sum(grad_one, axis=0),
            jnp.sum(grad_branch.astype(f32), axis=0),
            jnp.sum(grad_two * unit_two, axis=0),
            jnp.sum(grad_two, axis=0),
            jnp.sum(grad_rows, axis=0),
        ]
    )
    sums = lax.psum(sums, ("f", "z", "c")) * scaling
    sums = lax.dynamic_index_in_dim(sums.reshape(6, columns, -1), me_f, 1, keepdims=False)
    wide = jnp.concatenate(
        [
            jnp.sum(grad_hidden.astype(f32), axis=0),
            jnp.sum(dq.astype(f32), axis=0),
            jnp.sum(dv.astype(f32), axis=0),
        ]
    )
    slots = jnp.where(jnp.arange(CORES)[:, None] == me_c, wide[None], 0.0)
    slots = lax.psum(slots, ("z", "c")) * scaling
    up_bias = slots[:, :ff].reshape(-1)
    in_bias = slots[:, ff:].reshape(CORES, 2, group).transpose(1, 0, 2).reshape(2, -1)

    return (
        layer_output[None],
        input_gradient[None],
        sums[0],
        sums[1],
        in_gradient,
        in_bias,
        out_gradient,
        sums[2],
        sums[3],
        sums[4],
        up_gradient,
        up_bias,
        down_gradient,
        sums[5],
    )


def solution(mesh):
    columns, seq = mesh.devices.shape
    split = Mesh(mesh.devices.reshape(columns, seq // CORES, CORES), ("f", "z", "c"))
    rows = P("f", ("z", "c"), None)
    vector, matrix, paired = P("f"), P("f", None), P(None, "f")
    return jax.shard_map(
        local,
        mesh=split,
        in_specs=(
            rows,
            P("f", None),
            rows,
            vector,
            vector,
            matrix,
            paired,
            matrix,
            vector,
            vector,
            vector,
            matrix,
            vector,
            matrix,
            vector,
        ),
        out_specs=(
            rows,
            rows,
            vector,
            vector,
            matrix,
            paired,
            matrix,
            vector,
            vector,
            vector,
            matrix,
            vector,
            matrix,
            vector,
        ),
        check_vma=False,
    )
```

```python
import functools

import jax
import jax.numpy as jnp
from jax import lax
from jax.experimental import pallas as pl
from jax.experimental.pallas import tpu as pltpu
from jax.sharding import Mesh, PartitionSpec as P

HEADS = 32
HEAD_DIM = 64
BLOCK = 128
DOCS = 4
TILE = 256
CORES = 2
MASKED = -1e30

epsilon = 1e-05
bf16 = jnp.bfloat16
f32 = jnp.float32


def contract(a, b, da, db):
    return lax.dot_general(a, b, (((da,), (db,)), ((), ())), preferred_element_type=f32)


def tile_bias(bias_ref, slope_ref, pair):
    keys = lax.broadcasted_iota(jnp.int32, (TILE, TILE), 0)
    queries = lax.broadcasted_iota(jnp.int32, (TILE, TILE), 1)
    gap = (keys - queries).astype(f32)
    for h in range(2):
        bias_ref[h] = gap * slope_ref[pair * 2 + h]


def head_halves(block):
    lane = lax.broadcasted_iota(jnp.int32, block.shape, 1)
    zero = jnp.zeros_like(block)
    return [jnp.where((lane // HEAD_DIM) == h, block, zero) for h in range(2)]


def forward_kernel(
    first_ref, slope_ref, q_ref, k_ref, v_ref, low_ref, high_ref, out_ref, lse_ref, vt_ref, bias_ref
):
    pair, qi = pl.program_id(0), pl.program_id(1)

    @pl.when(qi == 0)
    def _():
        vt_ref[...] = v_ref[...].T
        tile_bias(bias_ref, slope_ref, pair)

    queries = head_halves(q_ref[...] * jnp.asarray(HEAD_DIM**-0.5, bf16))
    low, high = low_ref[...], high_ref[...]
    rows = lax.broadcasted_iota(jnp.int32, (TILE, TILE), 0)
    here = pl.multiple_of(qi * TILE, TILE)
    diagonal = k_ref[pl.ds(here, TILE), :]
    inside = (rows >= low - here) & (rows < high - here)
    state = []
    for h in range(2):
        scores = contract(diagonal, queries[h], 1, 1) - jnp.abs(bias_ref[h])
        scores = jnp.where(inside, scores, MASKED)
        peak = jnp.max(scores, axis=0, keepdims=True)
        weights = jnp.exp(scores - peak)
        total = jnp.sum(weights, axis=0, keepdims=True)
        values = vt_ref[pl.ds(h * HEAD_DIM, HEAD_DIM), pl.ds(here, TILE)]
        state += [peak, total, contract(values, weights.astype(bf16), 1, 0)]

    def step(t, state):
        start = pl.multiple_of(t * TILE, TILE)
        keys = k_ref[pl.ds(start, TILE), :]
        seen = rows >= low - start
        away = ((t - qi) * TILE).astype(f32)
        fresh = []
        for h in range(2):
            peak, total, mixed = state[3 * h : 3 * h + 3]
            scores = contract(keys, queries[h], 1, 1) + bias_ref[h]
            scores = jnp.where(seen, scores, MASKED)
            offset = away * slope_ref[pair * 2 + h]
            top = jnp.maximum(peak, jnp.max(scores, axis=0, keepdims=True) + offset)
            weights = jnp.exp(scores + (offset - top))
            shrink = jnp.exp(peak - top)
            values = vt_ref[pl.ds(h * HEAD_DIM, HEAD_DIM), pl.ds(start, TILE)]
            fresh += [
                top,
                total * shrink + jnp.sum(weights, axis=0, keepdims=True),
                mixed * shrink + contract(values, weights.astype(bf16), 1, 0),
            ]
        return tuple(fresh)

    state = lax.fori_loop(first_ref[qi], qi, step, tuple(state))
    mixed = jnp.concatenate([state[2] / state[1], state[5] / state[4]], axis=0)
    out_ref[...] = mixed.T.astype(bf16)
    lse_ref[0] = jnp.concatenate([state[0] + jnp.log(state[1]), state[3] + jnp.log(state[4])], axis=0)


def backward_kernel(
    first_ref,
    slope_ref,
    q_ref,
    k_ref,
    v_ref,
    out_ref,
    grad_ref,
    lse_ref,
    low_ref,
    high_ref,
    dq_ref,
    dk_ref,
    dv_ref,
    kt_ref,
    bias_ref,
    dk_sum,
    dv_sum,
    dq_sum,
):
    pair, qi = pl.program_id(0), pl.program_id(1)

    @pl.when(qi == 0)
    def _():
        kt_ref[...] = k_ref[...].T
        tile_bias(bias_ref, slope_ref, pair)
        dk_sum[...] = jnp.zeros_like(dk_sum)
        dv_sum[...] = jnp.zeros_like(dv_sum)

    queries = head_halves(q_ref[...] * jnp.asarray(HEAD_DIM**-0.5, bf16))
    grads = head_halves(grad_ref[...])
    low, high = low_ref[...], high_ref[...]
    rows = lax.broadcasted_iota(jnp.int32, (TILE, TILE), 0)
    product = (grad_ref[...].astype(f32) * out_ref[...].astype(f32)).T
    deltas = [
        jnp.sum(product[h * HEAD_DIM : (h + 1) * HEAD_DIM], axis=0, keepdims=True) for h in range(2)
    ]
    lse = [lse_ref[0, pl.ds(h, 1), :] for h in range(2)]
    dq_sum[...] = jnp.zeros_like(dq_sum)

    def tile(start, on_diagonal, offsets):
        keys = k_ref[pl.ds(start, TILE), :]
        values = v_ref[pl.ds(start, TILE), :]
        seen = rows >= low - start
        if on_diagonal:
            seen = seen & (rows < high - start)
        dk, dv = dk_sum[pl.ds(start, TILE), :], dv_sum[pl.ds(start, TILE), :]
        for h in range(2):
            scores = contract(keys, queries[h], 1, 1)
            if on_diagonal:
                scores = scores - jnp.abs(bias_ref[h]) - lse[h]
            else:
                scores = scores + bias_ref[h] + (offsets[h] - lse[h])
            probs = jnp.exp(jnp.where(seen, scores, MASKED))
            pull = contract(values, grads[h], 1, 1)
            grad_scores = (probs * (pull - deltas[h])).astype(bf16)
            dv = dv + contract(probs.astype(bf16), grads[h], 1, 0)
            dk = dk + contract(grad_scores, queries[h], 1, 0)
            keys_t = kt_ref[pl.ds(h * HEAD_DIM, HEAD_DIM), pl.ds(start, TILE)]
            dq_sum[pl.ds(h * HEAD_DIM, HEAD_DIM), :] += contract(keys_t, grad_scores, 1, 0)
        dk_sum[pl.ds(start, TILE), :] = dk
        dv_sum[pl.ds(start, TILE), :] = dv

    tile(pl.multiple_of(qi * TILE, TILE), True, None)

    def step(t, carry):
        away = ((t - qi) * TILE).astype(f32)
        tile(
            pl.multiple_of(t * TILE, TILE),
            False,
            [away * slope_ref[pair * 2 + h] for h in range(2)],
        )
        return carry

    lax.fori_loop(first_ref[qi], qi, step, 0)
    dq_ref[...] = (dq_sum[...] * HEAD_DIM**-0.5).T.astype(bf16)

    @pl.when(qi == pl.num_programs(1) - 1)
    def _():
        dk_ref[...] = dk_sum[...].astype(bf16)
        dv_ref[...] = dv_sum[...].astype(bf16)


def attention_specs(length, pairs):
    wide = 2 * HEAD_DIM

    def tiles(third):
        return pl.BlockSpec((TILE, wide), lambda p, i, *_: (i, third * pairs + p))

    def whole(third):
        return pl.BlockSpec((length, wide), lambda p, i, *_: (0, third * pairs + p))

    limits = pl.BlockSpec((1, TILE), lambda p, i, *_: (0, i))
    lse = pl.BlockSpec((1, 2, TILE), lambda p, i, *_: (p, 0, i))
    return tiles, whole, limits, lse


def attention(stacked, low, high, first, slopes):
    length, pairs = stacked.shape[0], stacked.shape[1] // (6 * HEAD_DIM)
    tiles, whole, limits, lse = attention_specs(length, pairs)
    return pl.pallas_call(
        forward_kernel,
        grid_spec=pltpu.PrefetchScalarGridSpec(
            num_scalar_prefetch=2,
            grid=(pairs, length // TILE),
            in_specs=[tiles(0), whole(1), whole(2), limits, limits],
            out_specs=[tiles(0), lse],
            scratch_shapes=[
                pltpu.VMEM((2 * HEAD_DIM, length), bf16),
                pltpu.VMEM((2, TILE, TILE), f32),
            ],
        ),
        out_shape=[
            jax.ShapeDtypeStruct((length, pairs * 2 * HEAD_DIM), bf16),
            jax.ShapeDtypeStruct((pairs, 2, length), f32),
        ],
        compiler_params=pltpu.CompilerParams(vmem_limit_bytes=32 << 20),
        cost_estimate=pl.CostEstimate(
            flops=16_000_000_000, bytes_accessed=8 << 20, transcendentals=8 << 20
        ),
        name="attention_forward",
    )(first, slopes, stacked, stacked, stacked, low, high)


def attention_back(stacked, mixed, grads, lse_rows, low, high, first, slopes):
    length, pairs = stacked.shape[0], stacked.shape[1] // (6 * HEAD_DIM)
    tiles, whole, limits, lse = attention_specs(length, pairs)
    shape = jax.ShapeDtypeStruct((length, pairs * 2 * HEAD_DIM), bf16)
    return pl.pallas_call(
        backward_kernel,
        grid_spec=pltpu.PrefetchScalarGridSpec(
            num_scalar_prefetch=2,
            grid=(pairs, length // TILE),
            in_specs=[tiles(0), whole(1), whole(2), tiles(0), tiles(0), lse, limits, limits],
            out_specs=[tiles(0), whole(0), whole(0)],
            scratch_shapes=[
                pltpu.VMEM((2 * HEAD_DIM, length), bf16),
                pltpu.VMEM((2, TILE, TILE), f32),
                pltpu.VMEM((length, 2 * HEAD_DIM), f32),
                pltpu.VMEM((length, 2 * HEAD_DIM), f32),
                pltpu.VMEM((2 * HEAD_DIM, TILE), f32),
            ],
        ),
        out_shape=[shape, shape, shape],
        compiler_params=pltpu.CompilerParams(vmem_limit_bytes=32 << 20),
        cost_estimate=pl.CostEstimate(
            flops=40_000_000_000, bytes_accessed=16 << 20, transcendentals=8 << 20
        ),
        name="attention_backward",
    )(first, slopes, stacked, stacked, stacked, mixed, grads, lse_rows, low, high)


def moments(values):
    centre = jnp.mean(values, axis=-1, keepdims=True)
    offset = values - centre
    rate = lax.rsqrt(jnp.mean(offset * offset, axis=-1, keepdims=True) + epsilon)
    return offset * rate, rate


def norm_back(grads, unit, rate, gain):
    scaled = grads * gain
    mean = jnp.mean(scaled, axis=-1, keepdims=True)
    along = jnp.mean(scaled * unit, axis=-1, keepdims=True)
    return rate * (scaled - mean - unit * along)


def dot(a, b):
    return jnp.dot(a, b, preferred_element_type=f32)


def gelu_parts(values):
    phi = 0.5 * (1.0 + lax.erf(values * (0.5**0.5)))
    density = jnp.exp(-0.5 * values * values) * 0.3989422804014327
    return values * phi, phi + values * density


def pick(values, index, axis):
    return lax.dynamic_index_in_dim(values, index, axis, keepdims=False)


def put(values, piece, *index):
    return lax.dynamic_update_slice(values, piece, index)


def send(values, axis, distance):
    n = lax.axis_size(axis)
    return lax.ppermute(values, axis, [(i, i ^ distance) for i in range(n)])


def butterfly(values, axes):
    for axis in axes:
        distance = 1
        while distance < lax.axis_size(axis):
            values = values + send(values, axis, distance)
            distance *= 2
    return values


def to_planes(rows):
    n = lax.axis_size("f")
    me_f, me_z = lax.axis_index("f"), lax.axis_index("z")
    split = rows.reshape((n, -1) + rows.shape[1:])
    zeros = (0,) * rows.ndim
    held = jnp.zeros_like(split)
    for d in range(n):
        piece = pick(split, me_f ^ d, 0)
        piece = send(piece, "f", d) if d else piece
        held = put(held, piece[None], me_f ^ d, *zeros)
    out = jnp.zeros_like(split)
    for e in range(lax.axis_size("z")):
        piece = pick(held, me_z ^ e, 0)
        piece = send(piece, "z", e) if e else piece
        out = put(out, piece[None], me_z ^ e, *zeros)
    return out


def from_planes(blocks):
    n = lax.axis_size("f")
    me_f, me_z = lax.axis_index("f"), lax.axis_index("z")
    zeros = (0,) * (blocks.ndim - 1)
    held = jnp.zeros_like(blocks)
    for e in range(lax.axis_size("z")):
        piece = pick(blocks, me_z ^ e, 0)
        piece = send(piece, "z", e) if e else piece
        held = put(held, piece[None], me_z ^ e, *zeros)
    out = jnp.zeros_like(blocks)
    for d in range(n):
        piece = pick(held, me_f ^ d, 0)
        piece = send(piece, "f", d) if d else piece
        out = put(out, piece[None], me_f ^ d, *zeros)
    return out.reshape((-1,) + blocks.shape[2:])


def plane_gather(own):
    n = lax.axis_size("f")
    me_f, me_c = lax.axis_index("f"), lax.axis_index("c")
    blocks, part, width = own.shape
    half = blocks // 2
    pieces = [(own, 0, 0)]
    if n == 4:
        along_x, along_y = send(own, "f", 1), send(own, "f", 2)
        pieces += [(along_x, 1, 0), (along_y, 2, 0)]
        pieces += [(send(along_x[:half], "f", 2), 3, 0), (send(along_y[half:], "f", 1), 3, half)]
    else:
        pieces += [(send(own, "f", d), d, 0) for d in range(1, n)]
    full = jnp.zeros((blocks, CORES, n, part, width), own.dtype)
    for piece, distance, block in pieces:
        other = send(piece, "c", 1)
        full = put(full, piece[:, None, None], block, me_c, me_f ^ distance, 0, 0)
        full = put(full, other[:, None, None], block, 1 - me_c, me_f ^ distance, 0, 0)
    return full.reshape(-1, width)


def plane_scatter(partial, blocks):
    n = lax.axis_size("f")
    me_f, me_c = lax.axis_index("f"), lax.axis_index("c")
    width = partial.shape[-1]
    split = partial.reshape(blocks, CORES, n, -1, width)
    part = split.shape[3]
    half = blocks // 2

    def block(core, distance):
        size = (blocks, 1, 1, part, width)
        piece = lax.dynamic_slice(split, (0, core, me_f ^ distance, 0, 0), size)
        return piece.reshape(blocks, part, width)

    sums = {}
    for d in list(range(n - 1, 0, -1)) + [0]:
        other = send(block(1 - me_c, d), "c", 1)
        sums[d] = block(me_c, d).astype(f32) + other.astype(f32)
    if n == 4:
        far = sums[3].astype(bf16)
        for_y, for_x = send(far[:half], "f", 1), send(far[half:], "f", 2)
        near_x = jnp.concatenate([sums[1][:half], sums[1][half:] + for_x.astype(f32)])
        near_y = jnp.concatenate([sums[2][:half] + for_y.astype(f32), sums[2][half:]])
        from_x, from_y = send(near_x.astype(bf16), "f", 1), send(near_y.astype(bf16), "f", 2)
        return sums[0] + from_x.astype(f32) + from_y.astype(f32)
    total = sums[0]
    for d in range(1, n):
        total = total + send(sums[d].astype(bf16), "f", d).astype(f32)
    return total


def heads_to_tokens(mixed, blocks):
    n = lax.axis_size("f")
    me_f, me_c = lax.axis_index("f"), lax.axis_index("c")
    group = mixed.shape[-1]
    split = mixed.reshape(blocks, CORES, n, -1, group)
    mine = pick(split, me_c, 1)
    other = send(pick(split, 1 - me_c, 1), "c", 1)
    both = jnp.where(
        me_c == 0, jnp.concatenate([mine, other], -1), jnp.concatenate([other, mine], -1)
    )
    part = both.shape[2]
    full = jnp.zeros((blocks, part, n, CORES * group), mixed.dtype)
    for d in range(n):
        piece = pick(both, me_f ^ d, 1)
        piece = send(piece, "f", d) if d else piece
        full = put(full, piece[:, :, None], 0, 0, me_f ^ d, 0)
    return full.reshape(blocks, part, -1)


def tokens_to_heads(rows, blocks):
    n = lax.axis_size("f")
    me_f, me_c = lax.axis_index("f"), lax.axis_index("c")
    part = rows.shape[1]
    split = rows.reshape(blocks, part, n, CORES, -1)
    group = split.shape[-1]
    both = jnp.zeros((blocks, n, part, CORES, group), rows.dtype)
    for d in range(n):
        piece = pick(split, me_f ^ d, 2)
        piece = send(piece, "f", d) if d else piece
        both = put(both, piece[:, None], 0, me_f ^ d, 0, 0, 0)
    mine = pick(both, me_c, 3)
    other = send(pick(both, 1 - me_c, 3), "c", 1)
    full = jnp.where(me_c == 0, jnp.stack([mine, other], 1), jnp.stack([other, mine], 1))
    return full.reshape(-1, group)


def local(
    inputs,
    documents,
    cotangent,
    attend_gain,
    attend_shift,
    project_in,
    project_bias,
    project_out,
    output_bias,
    feed_gain,
    feed_shift,
    expand_weight,
    expand_bias,
    reduce_weight,
    reduce_bias,
):
    columns, planes = lax.axis_size("f"), lax.axis_size("z")
    me_f, me_z, me_c = lax.axis_index("f"), lax.axis_index("z"), lax.axis_index("c")
    width = inputs.shape[2]
    length = documents.shape[1]
    hidden = expand_weight.shape[1]
    device_heads = HEADS // (columns * CORES)
    group = device_heads * HEAD_DIM
    ff = hidden // (columns * CORES)
    unit = ff // planes
    scaling = (columns * length) ** (-0.5)

    tokens = to_planes(inputs[0])
    turn = [(a * planes + b, b * planes + a) for a in range(columns) for b in range(planes)]
    docs = lax.ppermute(documents, ("f", "z"), turn)
    grad_own = to_planes(cotangent[0])

    vectors = jnp.stack([attend_gain, attend_shift, output_bias, feed_gain, feed_shift, reduce_bias])
    vectors = lax.all_gather(vectors, "f", axis=1, tiled=True).astype(f32)
    gain_one, shift_one, bias_out, gain_two, shift_two, bias_reduce = vectors

    thirds = pick(project_in.reshape(-1, 3, columns, CORES, group), me_c, 3)
    weight_in = jnp.zeros((columns,) + thirds.shape[:2] + (group,), bf16)
    for d in range(columns):
        piece = pick(thirds, me_f ^ d, 2)
        piece = send(piece, "f", d) if d else piece
        weight_in = put(weight_in, piece[None], me_f ^ d, 0, 0, 0)
    weight_in = weight_in.reshape(width, 3 * group)
    some = project_out.shape[0] // (planes * CORES)
    mine = lax.dynamic_slice_in_dim(project_out, (me_z * CORES + me_c) * some, some)
    weight_out = lax.all_gather(mine, ("f", "z", "c"), axis=0, tiled=True)
    strip = expand_weight.shape[0] // planes
    slices = lax.dynamic_slice_in_dim(expand_weight, me_z * strip, strip)
    slices = pick(slices.reshape(strip, columns, planes, CORES, unit), me_c, 3)
    slices = slices.reshape(strip, columns, ff)
    weight_up = jnp.zeros((columns, strip, ff), bf16)
    for d in range(columns):
        piece = pick(slices, me_f ^ d, 1)
        piece = send(piece, "f", d) if d else piece
        weight_up = put(weight_up, piece[None], me_f ^ d, 0, 0)
    weight_up = lax.all_gather(weight_up, "z", axis=0, tiled=False)
    weight_up = weight_up.transpose(1, 0, 2, 3).reshape(width, ff)
    weight_down = pick(reduce_weight.reshape(planes, CORES, unit, width), me_c, 1).reshape(ff, width)
    bias_pair = pick(project_bias.reshape(2, CORES, group), me_c, 1).astype(f32)
    bias_in = jnp.concatenate([bias_pair[0], jnp.zeros((group,), f32), bias_pair[1]])
    bias_up = pick(expand_bias.reshape(planes, CORES, unit), me_c, 1).reshape(ff).astype(f32)

    doc_row = docs[0]
    position = jnp.arange(length, dtype=jnp.int32)
    low = jnp.zeros_like(doc_row)
    end = jnp.zeros_like(doc_row)
    for d in range(DOCS):
        low = jnp.where(doc_row == d, jnp.sum((doc_row < d).astype(jnp.int32)), low)
        end = jnp.where(doc_row == d, jnp.sum((doc_row <= d).astype(jnp.int32)), end)
    high = jnp.minimum(end, (position // BLOCK + 1) * BLOCK)
    first = low[::TILE] // TILE
    low, high = low[None], high[None]
    first_head = (me_f * CORES + me_c) * device_heads
    heads = first_head + 1 + jnp.arange(device_heads, dtype=jnp.int32)
    slopes = 2.0 ** (-8.0 * heads.astype(f32) / HEADS)

    token_rows = tokens.astype(f32)
    unit_one, rate_one = moments(token_rows)
    normed_one = plane_gather((unit_one * gain_one + shift_one).astype(bf16))
    stacked = (dot(normed_one, weight_in) + bias_in).astype(bf16)
    mixed, lse_rows = attention(stacked, low, high, first, slopes)
    mixed_own = heads_to_tokens(mixed, planes)
    middle = token_rows + (dot(mixed_own, weight_out) + bias_out)
    unit_two, rate_two = moments(middle)
    normed_two = plane_gather((unit_two * gain_two + shift_two).astype(bf16))
    hidden_pre = dot(normed_two, weight_up) + bias_up
    active, slope = gelu_parts(hidden_pre)
    active = active.astype(bf16)

    grad_all = plane_gather(grad_own)
    down_term = contract(active, grad_all, 0, 0).astype(bf16)
    down_share = lax.psum_scatter(down_term, "z", scatter_dimension=0, tiled=True)
    grad_active = contract(grad_all, weight_down, 1, 1)
    grad_hidden = (grad_active * slope).astype(bf16)
    grad_two = plane_scatter(contract(grad_hidden, weight_up, 1, 1).astype(bf16), planes)
    up_term = contract(normed_two, grad_hidden, 0, 0).astype(bf16)

    def share_rows(term):
        part = lax.psum_scatter(
            term.reshape(columns, -1, term.shape[-1]), "z", scatter_dimension=1, tiled=True
        )
        part = part.reshape(columns * CORES, -1, term.shape[-1])
        return lax.all_to_all(part, ("f", "c"), split_axis=0, concat_axis=0, tiled=True)

    up_share = share_rows(up_term)
    up_share = up_share.reshape(columns, CORES, -1, planes, unit).transpose(2, 0, 3, 1, 4)
    up_share = up_share.reshape(-1, hidden)

    grad_rows = grad_own.astype(f32)
    grad_middle = grad_rows + norm_back(grad_two, unit_two, rate_two, gain_two)
    grad_branch = grad_middle.astype(bf16)
    grad_mixed_own = lax.dot_general(
        grad_branch, weight_out, (((2,), (1,)), ((), ())), preferred_element_type=f32
    )
    grad_mixed = tokens_to_heads(grad_mixed_own.astype(bf16), planes)
    branch_all = plane_gather(grad_branch)
    out_term = contract(mixed, branch_all, 0, 0).astype(bf16)
    out_share = lax.psum_scatter(out_term, "z", scatter_dimension=0, tiled=True)

    forward_sum = plane_scatter(dot(active, weight_down).astype(bf16), planes)
    layer_output = from_planes((middle + forward_sum + bias_reduce).astype(bf16))

    dq, dk, dv = attention_back(stacked, mixed, grad_mixed, lse_rows, low, high, first, slopes)
    grad_projected = jnp.concatenate([dq, dk, dv], axis=1)
    grad_one = plane_scatter(contract(grad_projected, weight_in, 1, 1).astype(bf16), planes)
    in_term = contract(normed_one, grad_projected, 0, 0).astype(bf16)
    in_share = share_rows(in_term)
    in_share = in_share.reshape(columns, CORES, -1, 3, group).transpose(2, 3, 0, 1, 4)
    in_share = in_share.reshape(-1, 3 * width)
    input_rows = grad_middle + norm_back(grad_one, unit_one, rate_one, gain_one)
    input_gradient = from_planes(input_rows.astype(bf16)).astype(f32)

    def spread(share):
        return lax.all_gather(share, ("z", "c"), axis=0, tiled=True).astype(f32) * scaling

    down_gradient = spread(down_share)
    up_gradient = spread(up_share)
    in_gradient = spread(in_share)
    out_all = lax.all_gather(out_share, ("z", "c"), axis=0, tiled=False)
    out_all = out_all.reshape((planes, CORES) + out_share.shape).transpose(1, 0, 2, 3)
    out_gradient = out_all.reshape(-1, width).astype(f32) * scaling

    def own_part(sums):
        sums = butterfly(sums, ("c", "f", "z")) * scaling
        return pick(sums.reshape(sums.shape[0], columns, -1), me_f, 1)

    def total(values):
        return jnp.sum(values, axis=(0, 1))

    second = own_part(
        jnp.stack(
            [
                total(grad_branch.astype(f32)),
                total(grad_two * unit_two),
                total(grad_two),
                total(grad_rows),
            ]
        )
    )
    first_pair = own_part(jnp.stack([total(grad_one * unit_one), total(grad_one)]))
    up_bias = butterfly(jnp.sum(grad_hidden.astype(f32), axis=0), ("z",)) * scaling
    up_bias = up_bias.reshape(planes, unit)
    in_bias = jnp.stack([jnp.sum(dq.astype(f32), axis=0), jnp.sum(dv.astype(f32), axis=0)])
    in_bias = butterfly(in_bias, ("z",)) * scaling

    def both_cores(mine):
        other = send(mine, "c", 1)
        return jnp.where(me_c == 0, jnp.stack([mine, other], 1), jnp.stack([other, mine], 1))

    up_bias = both_cores(up_bias).reshape(-1)
    in_bias = both_cores(in_bias).reshape(2, -1)

    return (
        layer_output[None],
        input_gradient[None],
        first_pair[0],
        first_pair[1],
        in_gradient,
        in_bias,
        out_gradient,
        second[0],
        second[1],
        second[2],
        up_gradient,
        up_bias,
        down_gradient,
        second[3],
    )


def solution(mesh):
    columns, seq = mesh.devices.shape
    split = Mesh(mesh.devices.reshape(columns, seq // CORES, CORES), ("f", "z", "c"))
    rows = P("f", ("z", "c"), None)
    vector, matrix, paired = P("f"), P("f", None), P(None, "f")
    return jax.shard_map(
        local,
        mesh=split,
        in_specs=(
            rows,
            P("f", None),
            rows,
            vector,
            vector,
            matrix,
            paired,
            matrix,
            vector,
            vector,
            vector,
            matrix,
            vector,
            matrix,
            vector,
        ),
        out_specs=(
            rows,
            rows,
            vector,
            vector,
            matrix,
            paired,
            matrix,
            vector,
            vector,
            vector,
            matrix,
            vector,
            matrix,
            vector,
        ),
        check_vma=False,
    )
```

```python
import functools

import jax
import jax.numpy as jnp
from jax import lax
from jax.experimental import pallas as pl
from jax.experimental.pallas import tpu as pltpu
from jax.sharding import Mesh, PartitionSpec as P

HEADS = 32
HEAD_DIM = 64
BLOCK = 128
DOCS = 4
TILE = 256
CORES = 2
MASKED = -1e30

epsilon = 1e-05
bf16 = jnp.bfloat16
f32 = jnp.float32


def contract(a, b, da, db):
    return lax.dot_general(a, b, (((da,), (db,)), ((), ())), preferred_element_type=f32)


def tile_bias(bias_ref, slope_ref, pair):
    keys = lax.broadcasted_iota(jnp.int32, (TILE, TILE), 0)
    queries = lax.broadcasted_iota(jnp.int32, (TILE, TILE), 1)
    gap = (keys - queries).astype(f32)
    for h in range(2):
        bias_ref[h] = gap * slope_ref[pair * 2 + h]


def head_halves(block):
    lane = lax.broadcasted_iota(jnp.int32, block.shape, 1)
    zero = jnp.zeros_like(block)
    return [jnp.where((lane // HEAD_DIM) == h, block, zero) for h in range(2)]


def forward_kernel(
    first_ref, slope_ref, q_ref, k_ref, v_ref, low_ref, high_ref, out_ref, lse_ref, vt_ref, bias_ref
):
    pair, qi = pl.program_id(0), pl.program_id(1)

    @pl.when(qi == 0)
    def _():
        vt_ref[...] = v_ref[...].T
        tile_bias(bias_ref, slope_ref, pair)

    queries = head_halves(q_ref[...] * jnp.asarray(HEAD_DIM**-0.5, bf16))
    low, high = low_ref[...], high_ref[...]
    rows = lax.broadcasted_iota(jnp.int32, (TILE, TILE), 0)
    here = pl.multiple_of(qi * TILE, TILE)
    diagonal = k_ref[pl.ds(here, TILE), :]
    inside = (rows >= low - here) & (rows < high - here)
    state = []
    for h in range(2):
        scores = contract(diagonal, queries[h], 1, 1) - jnp.abs(bias_ref[h])
        scores = jnp.where(inside, scores, MASKED)
        peak = jnp.max(scores, axis=0, keepdims=True)
        weights = jnp.exp(scores - peak)
        total = jnp.sum(weights, axis=0, keepdims=True)
        values = vt_ref[pl.ds(h * HEAD_DIM, HEAD_DIM), pl.ds(here, TILE)]
        state += [peak, total, contract(values, weights.astype(bf16), 1, 0)]

    def step(t, state):
        start = pl.multiple_of(t * TILE, TILE)
        keys = k_ref[pl.ds(start, TILE), :]
        seen = rows >= low - start
        away = ((t - qi) * TILE).astype(f32)
        fresh = []
        for h in range(2):
            peak, total, mixed = state[3 * h : 3 * h + 3]
            scores = contract(keys, queries[h], 1, 1) + bias_ref[h]
            scores = jnp.where(seen, scores, MASKED)
            offset = away * slope_ref[pair * 2 + h]
            top = jnp.maximum(peak, jnp.max(scores, axis=0, keepdims=True) + offset)
            weights = jnp.exp(scores + (offset - top))
            shrink = jnp.exp(peak - top)
            values = vt_ref[pl.ds(h * HEAD_DIM, HEAD_DIM), pl.ds(start, TILE)]
            fresh += [
                top,
                total * shrink + jnp.sum(weights, axis=0, keepdims=True),
                mixed * shrink + contract(values, weights.astype(bf16), 1, 0),
            ]
        return tuple(fresh)

    state = lax.fori_loop(first_ref[qi], qi, step, tuple(state))
    mixed = jnp.concatenate([state[2] / state[1], state[5] / state[4]], axis=0)
    out_ref[...] = mixed.T.astype(bf16)
    lse_ref[0] = jnp.concatenate([state[0] + jnp.log(state[1]), state[3] + jnp.log(state[4])], axis=0)


def backward_kernel(
    first_ref,
    slope_ref,
    q_ref,
    k_ref,
    v_ref,
    out_ref,
    grad_ref,
    lse_ref,
    low_ref,
    high_ref,
    dq_ref,
    dk_ref,
    dv_ref,
    kt_ref,
    bias_ref,
    dk_sum,
    dv_sum,
    dq_sum,
):
    pair, qi = pl.program_id(0), pl.program_id(1)

    @pl.when(qi == 0)
    def _():
        kt_ref[...] = k_ref[...].T
        tile_bias(bias_ref, slope_ref, pair)
        dk_sum[...] = jnp.zeros_like(dk_sum)
        dv_sum[...] = jnp.zeros_like(dv_sum)

    queries = head_halves(q_ref[...] * jnp.asarray(HEAD_DIM**-0.5, bf16))
    grads = head_halves(grad_ref[...])
    low, high = low_ref[...], high_ref[...]
    rows = lax.broadcasted_iota(jnp.int32, (TILE, TILE), 0)
    product = (grad_ref[...].astype(f32) * out_ref[...].astype(f32)).T
    deltas = [
        jnp.sum(product[h * HEAD_DIM : (h + 1) * HEAD_DIM], axis=0, keepdims=True) for h in range(2)
    ]
    lse = [lse_ref[0, pl.ds(h, 1), :] for h in range(2)]
    dq_sum[...] = jnp.zeros_like(dq_sum)

    def tile(start, on_diagonal, offsets):
        keys = k_ref[pl.ds(start, TILE), :]
        values = v_ref[pl.ds(start, TILE), :]
        seen = rows >= low - start
        if on_diagonal:
            seen = seen & (rows < high - start)
        dk, dv = dk_sum[pl.ds(start, TILE), :], dv_sum[pl.ds(start, TILE), :]
        for h in range(2):
            scores = contract(keys, queries[h], 1, 1)
            if on_diagonal:
                scores = scores - jnp.abs(bias_ref[h]) - lse[h]
            else:
                scores = scores + bias_ref[h] + (offsets[h] - lse[h])
            probs = jnp.exp(jnp.where(seen, scores, MASKED))
            pull = contract(values, grads[h], 1, 1)
            grad_scores = (probs * (pull - deltas[h])).astype(bf16)
            dv = dv + contract(probs.astype(bf16), grads[h], 1, 0)
            dk = dk + contract(grad_scores, queries[h], 1, 0)
            keys_t = kt_ref[pl.ds(h * HEAD_DIM, HEAD_DIM), pl.ds(start, TILE)]
            dq_sum[pl.ds(h * HEAD_DIM, HEAD_DIM), :] += contract(keys_t, grad_scores, 1, 0)
        dk_sum[pl.ds(start, TILE), :] = dk
        dv_sum[pl.ds(start, TILE), :] = dv

    tile(pl.multiple_of(qi * TILE, TILE), True, None)

    def step(t, carry):
        away = ((t - qi) * TILE).astype(f32)
        tile(
            pl.multiple_of(t * TILE, TILE),
            False,
            [away * slope_ref[pair * 2 + h] for h in range(2)],
        )
        return carry

    lax.fori_loop(first_ref[qi], qi, step, 0)
    dq_ref[...] = (dq_sum[...] * HEAD_DIM**-0.5).T.astype(bf16)

    @pl.when(qi == pl.num_programs(1) - 1)
    def _():
        dk_ref[...] = dk_sum[...].astype(bf16)
        dv_ref[...] = dv_sum[...].astype(bf16)


def attention_specs(length, pairs):
    wide = 2 * HEAD_DIM

    def tiles(third):
        return pl.BlockSpec((TILE, wide), lambda p, i, *_: (i, third * pairs + p))

    def whole(third):
        return pl.BlockSpec((length, wide), lambda p, i, *_: (0, third * pairs + p))

    limits = pl.BlockSpec((1, TILE), lambda p, i, *_: (0, i))
    lse = pl.BlockSpec((1, 2, TILE), lambda p, i, *_: (p, 0, i))
    return tiles, whole, limits, lse


def attention(stacked, low, high, first, slopes):
    length, pairs = stacked.shape[0], stacked.shape[1] // (6 * HEAD_DIM)
    tiles, whole, limits, lse = attention_specs(length, pairs)
    return pl.pallas_call(
        forward_kernel,
        grid_spec=pltpu.PrefetchScalarGridSpec(
            num_scalar_prefetch=2,
            grid=(pairs, length // TILE),
            in_specs=[tiles(0), whole(1), whole(2), limits, limits],
            out_specs=[tiles(0), lse],
            scratch_shapes=[
                pltpu.VMEM((2 * HEAD_DIM, length), bf16),
                pltpu.VMEM((2, TILE, TILE), f32),
            ],
        ),
        out_shape=[
            jax.ShapeDtypeStruct((length, pairs * 2 * HEAD_DIM), bf16),
            jax.ShapeDtypeStruct((pairs, 2, length), f32),
        ],
        compiler_params=pltpu.CompilerParams(vmem_limit_bytes=32 << 20),
        cost_estimate=pl.CostEstimate(
            flops=30_000_000_000, bytes_accessed=4 << 20, transcendentals=1 << 20
        ),
        name="attention_forward",
    )(first, slopes, stacked, stacked, stacked, low, high)


def attention_back(stacked, mixed, grads, lse_rows, low, high, first, slopes):
    length, pairs = stacked.shape[0], stacked.shape[1] // (6 * HEAD_DIM)
    tiles, whole, limits, lse = attention_specs(length, pairs)
    shape = jax.ShapeDtypeStruct((length, pairs * 2 * HEAD_DIM), bf16)
    return pl.pallas_call(
        backward_kernel,
        grid_spec=pltpu.PrefetchScalarGridSpec(
            num_scalar_prefetch=2,
            grid=(pairs, length // TILE),
            in_specs=[tiles(0), whole(1), whole(2), tiles(0), tiles(0), lse, limits, limits],
            out_specs=[tiles(0), whole(0), whole(0)],
            scratch_shapes=[
                pltpu.VMEM((2 * HEAD_DIM, length), bf16),
                pltpu.VMEM((2, TILE, TILE), f32),
                pltpu.VMEM((length, 2 * HEAD_DIM), f32),
                pltpu.VMEM((length, 2 * HEAD_DIM), f32),
                pltpu.VMEM((2 * HEAD_DIM, TILE), f32),
            ],
        ),
        out_shape=[shape, shape, shape],
        compiler_params=pltpu.CompilerParams(vmem_limit_bytes=32 << 20),
        cost_estimate=pl.CostEstimate(
            flops=30_000_000_000, bytes_accessed=8 << 20, transcendentals=1 << 20
        ),
        name="attention_backward",
    )(first, slopes, stacked, stacked, stacked, mixed, grads, lse_rows, low, high)


def moments(values):
    centre = jnp.mean(values, axis=-1, keepdims=True)
    offset = values - centre
    rate = lax.rsqrt(jnp.mean(offset * offset, axis=-1, keepdims=True) + epsilon)
    return offset * rate, rate


def norm_back(grads, unit, rate, gain):
    scaled = grads * gain
    mean = jnp.mean(scaled, axis=-1, keepdims=True)
    along = jnp.mean(scaled * unit, axis=-1, keepdims=True)
    return rate * (scaled - mean - unit * along)


def dot(a, b):
    return jnp.dot(a, b, preferred_element_type=f32)


def gelu_parts(values):
    phi = 0.5 * (1.0 + lax.erf(values * (0.5**0.5)))
    density = jnp.exp(-0.5 * values * values) * 0.3989422804014327
    return values * phi, phi + values * density


def pick(values, index, axis):
    return lax.dynamic_index_in_dim(values, index, axis, keepdims=False)


def put(values, piece, *index):
    return lax.dynamic_update_slice(values, piece, index)


def send(values, axis, distance):
    n = lax.axis_size(axis)
    return lax.ppermute(values, axis, [(i, i ^ distance) for i in range(n)])


def butterfly(values, axes):
    for axis in axes:
        distance = 1
        while distance < lax.axis_size(axis):
            values = values + send(values, axis, distance)
            distance *= 2
    return values


def tie(values, *others):
    for other in others:
        first = lax.slice(other, (0,) * other.ndim, (1,) * other.ndim).reshape(())
        values = values + (first.astype(f32) * 0.0).astype(values.dtype)
    return values


def exchange(values, axis):
    return lax.all_to_all(values, axis, split_axis=0, concat_axis=0, tiled=True)


def to_planes(rows):
    split = rows.reshape((lax.axis_size("f"), -1) + rows.shape[1:])
    return exchange(exchange(split, "f"), "z")


def from_planes(blocks):
    rows = exchange(exchange(blocks, "z"), "f")
    return rows.reshape((-1,) + blocks.shape[2:])


def by_position(values, blocks):
    split = values.reshape(lax.axis_size("f"), CORES, blocks, -1, values.shape[-1])
    return split.transpose(2, 1, 0, 3, 4).reshape(values.shape)


def by_owner(values, blocks):
    split = values.reshape(blocks, CORES, lax.axis_size("f"), -1, values.shape[-1])
    return split.transpose(2, 1, 0, 3, 4).reshape(values.shape)


def core_gather(own):
    n = lax.axis_size("f")
    half = own.shape[0] // 2
    if n != 4:
        return jnp.concatenate([own] + [send(own, "f", d) for d in range(1, n)])
    along_x, along_y = send(own, "f", 1), send(own, "f", 2)
    far = [send(along_x[:half], "f", 2), send(along_y[half:], "f", 1)]
    return jnp.concatenate([own, along_x, along_y] + far)


def plane_scatter(partial, *floor):
    n = lax.axis_size("f")
    me_f, me_c = lax.axis_index("f"), lax.axis_index("c")
    split = partial.reshape(n, CORES, -1, partial.shape[-1])
    half = split.shape[2] // 2
    other = send(tie(pick(split, 1 - me_c, 1), *floor), "c", 1)
    near = (pick(split, me_c, 1).astype(f32) + other.astype(f32)).astype(bf16)

    def block(distance):
        return pick(near, me_f ^ distance, 0)

    if n == 4:
        far = block(3)
        for_y, for_x = send(far[:half], "f", 1), send(far[half:], "f", 2)
        near_x, near_y = block(1), block(2)
        near_x = jnp.concatenate([near_x[:half], near_x[half:] + for_x])
        near_y = jnp.concatenate([near_y[:half] + for_y, near_y[half:]])
        from_x, from_y = send(near_x, "f", 1), send(near_y, "f", 2)
        return block(0).astype(f32) + from_x.astype(f32) + from_y.astype(f32)
    total = block(0).astype(f32)
    for d in range(1, n):
        total = total + send(block(d), "f", d).astype(f32)
    return total


def hop_in(values, *floor):
    if lax.axis_size("z") != 4:
        return lax.psum(values, "z")
    return tie(values, *floor) + lax.ppermute(values, "z", [(0, 1), (3, 2)])


def hop_across(near, *floor):
    if lax.axis_size("z") != 4:
        return near
    return tie(near, *floor) + lax.ppermute(near, "z", [(1, 2), (2, 1)])


def hop_out(total, *floor):
    if lax.axis_size("z") != 4:
        return total
    me_z = lax.axis_index("z")
    back = lax.ppermute(total, "z", [(1, 0), (2, 3)])
    return jnp.where((me_z == 0) | (me_z == 3), back, tie(total, *floor))


def core_rows(pieces):
    me_c = lax.axis_index("c")
    others = [send(piece, "c", 1) for piece in pieces]
    top = [jnp.where(me_c == 0, a, b).astype(f32) for a, b in zip(pieces, others)]
    bottom = [jnp.where(me_c == 0, b, a).astype(f32) for a, b in zip(pieces, others)]
    return jnp.concatenate(top + bottom)


def heads_to_tokens(mixed):
    devices = lax.axis_size("f") * CORES
    parts = exchange(mixed.reshape(devices, -1, mixed.shape[-1]), ("f", "c"))
    return parts.transpose(1, 0, 2).reshape(parts.shape[1], -1)


def tokens_to_heads(rows):
    devices = lax.axis_size("f") * CORES
    parts = rows.reshape(rows.shape[0], devices, -1).transpose(1, 0, 2)
    return exchange(parts, ("f", "c")).reshape(-1, parts.shape[-1])


def local(
    inputs,
    documents,
    cotangent,
    attend_gain,
    attend_shift,
    project_in,
    project_bias,
    project_out,
    output_bias,
    feed_gain,
    feed_shift,
    expand_weight,
    expand_bias,
    reduce_weight,
    reduce_bias,
):
    columns, planes = lax.axis_size("f"), lax.axis_size("z")
    me_f, me_z, me_c = lax.axis_index("f"), lax.axis_index("z"), lax.axis_index("c")
    width = inputs.shape[2]
    length = documents.shape[1]
    hidden = expand_weight.shape[1]
    device_heads = HEADS // (columns * CORES)
    group = device_heads * HEAD_DIM
    ff = hidden // (columns * CORES)
    unit = ff // planes
    scaling = (columns * length) ** (-0.5)

    vectors = jnp.stack([attend_gain, attend_shift, output_bias, feed_gain, feed_shift, reduce_bias])
    vectors = lax.all_gather(vectors, "f", axis=1, tiled=True).astype(f32)
    gain_one, shift_one, bias_out, gain_two, shift_two, bias_reduce = vectors

    split = tie(inputs[0], vectors).reshape(columns, -1, width)
    split = exchange(split, "f")
    tokens = exchange(split, "z").reshape(-1, width)
    turn = [(a * planes + b, b * planes + a) for a in range(columns) for b in range(planes)]
    docs = lax.ppermute(documents, ("f", "z"), turn)

    deep = project_in.shape[0]
    weight_in = jnp.zeros((width, 3 * group), bf16)
    for d in range(columns):
        column = ((me_f ^ d) * CORES + me_c) * group
        piece = jnp.concatenate(
            [
                lax.dynamic_slice(project_in, (0, third * width + column), (deep, group))
                for third in range(3)
            ],
            axis=1,
        )
        piece = send(piece, "f", d) if d else piece
        weight_in = put(weight_in, piece, (me_f ^ d) * deep, 0)
    grad_own = to_planes(tie(cotangent[0], tokens)).reshape(-1, width)
    strip = expand_weight.shape[0] // planes
    strips = lax.dynamic_slice_in_dim(expand_weight, me_z * strip, strip)
    turned = jnp.stack(
        [
            jnp.concatenate(
                [
                    lax.dynamic_slice(
                        strips, (0, (j * planes + p) * CORES * unit + me_c * unit), (strip, unit)
                    )
                    for p in range(planes)
                ],
                axis=1,
            )
            for j in range(columns)
        ]
    )
    turned = exchange(tie(turned, tokens), "f")
    up_pieces = [send(turned, "z", e) if e else turned for e in range(planes)]
    weight_down = pick(reduce_weight.reshape(planes, CORES, unit, width), me_c, 1).reshape(ff, width)
    bias_pair = pick(project_bias.reshape(2, CORES, group), me_c, 1).astype(f32)
    bias_in = jnp.concatenate([bias_pair[0], jnp.zeros((group,), f32), bias_pair[1]])
    bias_up = pick(expand_bias.reshape(planes, CORES, unit), me_c, 1).reshape(ff).astype(f32)

    doc_row = docs[0]
    position = jnp.arange(length, dtype=jnp.int32)
    low = jnp.zeros_like(doc_row)
    end = jnp.zeros_like(doc_row)
    for d in range(DOCS):
        low = jnp.where(doc_row == d, jnp.sum((doc_row < d).astype(jnp.int32)), low)
        end = jnp.where(doc_row == d, jnp.sum((doc_row <= d).astype(jnp.int32)), end)
    high = jnp.minimum(end, (position // BLOCK + 1) * BLOCK)
    first = low[::TILE] // TILE
    low, high = low[None], high[None]
    first_head = (me_f * CORES + me_c) * device_heads
    heads = first_head + 1 + jnp.arange(device_heads, dtype=jnp.int32)
    slopes = 2.0 ** (-8.0 * heads.astype(f32) / HEADS)

    token_rows = tie(tokens.astype(f32), weight_in)
    unit_one, rate_one = moments(token_rows)
    normed_one = (unit_one * gain_one + shift_one).astype(bf16)
    normed_one = lax.all_gather(normed_one, ("f", "c"), axis=0, tiled=True)
    stacked = tie(dot(normed_one, weight_in) + bias_in, grad_own, turned)
    stacked = by_position(stacked.astype(bf16), planes)
    mine = tie(pick(project_out.reshape(CORES, -1, width), me_c, 0), stacked)
    weight_out = lax.all_gather(mine, ("f", "c"), axis=0, tiled=True)
    mixed, lse_rows = attention(stacked, low, high, first, slopes)
    mixed_owned = by_owner(mixed, planes)
    weight_up = jnp.zeros((columns, planes, strip, ff), bf16)
    for e in range(planes):
        piece = up_pieces[e][:, None]
        weight_up = put(weight_up, piece, 0, me_z ^ e, 0, 0)
    weight_up = weight_up.reshape(width, ff)
    middle = token_rows + (dot(heads_to_tokens(mixed_owned), weight_out) + bias_out)
    unit_two, rate_two = moments(middle)
    grad_all = lax.all_gather(tie(grad_own, mixed), ("f", "c"), axis=0, tiled=True)
    normed_two = (unit_two * gain_two + shift_two).astype(bf16)
    normed_two = lax.all_gather(normed_two, ("f", "c"), axis=0, tiled=True)
    hidden_pre = dot(normed_two, weight_up) + bias_up
    active, slope = gelu_parts(hidden_pre)
    active = active.astype(bf16)

    down_term = contract(active, grad_all, 0, 0).astype(bf16)
    grad_active = tie(contract(grad_all, weight_down, 1, 1), down_term)
    grad_hidden = (grad_active * slope).astype(bf16)
    grad_partial = contract(grad_hidden, weight_up, 1, 1).astype(bf16)
    up_term = tie(contract(normed_two, grad_hidden, 0, 0), grad_partial).astype(bf16)
    forward_partial = tie(dot(active, weight_down), up_term).astype(bf16)
    down_share = lax.psum_scatter(down_term, "z", scatter_dimension=0, tiled=True)
    grad_two = tie(plane_scatter(grad_partial), up_term, forward_partial)
    up_share = up_term.reshape(columns, -1, ff)
    up_share = lax.psum_scatter(up_share, "z", scatter_dimension=1, tiled=True)

    grad_rows = grad_own.astype(f32)
    grad_middle = grad_rows + norm_back(grad_two, unit_two, rate_two, gain_two)
    grad_branch = grad_middle.astype(bf16)
    grad_mixed_owned = tokens_to_heads(contract(grad_branch, weight_out, 1, 1).astype(bf16))
    grad_mixed = tie(by_position(grad_mixed_owned, planes), down_share)
    branch_mine = core_gather(tie(grad_branch, grad_mixed_owned))
    branch_other = send(branch_mine, "c", 1)
    layer_sum = plane_scatter(forward_partial, grad_mixed_owned)
    dq, dk, dv = attention_back(stacked, mixed, grad_mixed, lse_rows, low, high, first, slopes)
    grad_projected = by_owner(jnp.concatenate([dq, dk, dv], axis=1), planes)
    grad_partial = contract(grad_projected, weight_in, 1, 1).astype(bf16)
    in_term = tie(contract(normed_one, grad_projected, 0, 0), grad_partial).astype(bf16)
    down_full = lax.all_gather(tie(down_share, dq), ("z", "c"), axis=0, tiled=True)
    grad_one = tie(plane_scatter(grad_partial), in_term, up_share)

    up_rows = tie(up_share, grad_one).reshape(columns * CORES, -1, ff)
    up_rows = exchange(up_rows, ("f", "c")).reshape(columns, CORES, -1, planes, unit)
    up_rows = up_rows.transpose(2, 0, 3, 1, 4).reshape(-1, hidden)
    up_full = lax.all_gather(up_rows, ("z", "c"), axis=0, tiled=True)

    turned = exchange(tie(in_term, up_rows).reshape(columns * CORES, -1, 3 * group), ("f", "c"))
    turned = turned.reshape(columns * CORES, -1, 3, group).transpose(1, 2, 0, 3)
    in_a, in_b = jnp.split(turned.reshape(-1, 3 * width), 2)
    input_rows = tie(grad_middle + norm_back(grad_one, unit_one, rate_one, gain_one), in_a)
    input_gradient = from_planes(input_rows.astype(bf16).reshape(planes, -1, width))
    mixed_cores = mixed_owned.reshape(columns, CORES, -1, group)

    def near_rows(core):
        rows = []
        for d in range(columns):
            size = (1, 1) + mixed_cores.shape[2:]
            rows.append(lax.dynamic_slice(mixed_cores, (me_f ^ d, core, 0, 0), size))
        return jnp.concatenate(rows).reshape(-1, group)

    out_term = contract(near_rows(me_c), branch_mine, 0, 0)
    out_term = (out_term + contract(near_rows(1 - me_c), branch_other, 0, 0)).astype(bf16)

    sums = jnp.stack(
        [
            jnp.sum(grad_one * unit_one, axis=0),
            jnp.sum(grad_one, axis=0),
            jnp.sum(grad_branch.astype(f32), axis=0),
            jnp.sum(grad_two * unit_two, axis=0),
            jnp.sum(grad_two, axis=0),
            jnp.sum(grad_rows, axis=0),
        ]
    )
    sums = butterfly(sums, ("c", "f"))
    biases = jnp.concatenate(
        [
            jnp.sum(grad_hidden.astype(f32), axis=0),
            jnp.sum(dq.astype(f32), axis=0),
            jnp.sum(dv.astype(f32), axis=0),
        ]
    )
    biases = jnp.pad(biases, (0, 2 * width - biases.shape[0])).reshape(2, width)
    out_term = jnp.concatenate([out_term, sums.astype(bf16), biases.astype(bf16)])
    near_a, near_b, near_out = hop_in(in_a, down_full), hop_in(in_b), hop_in(out_term)

    layer_rows = tie(middle + layer_sum + bias_reduce, input_gradient).astype(bf16)
    layer_output = from_planes(layer_rows.reshape(planes, -1, width))
    input_gradient = input_gradient.astype(f32)

    total_a, total_b, total_out = hop_across(near_a, up_full), hop_across(near_b), hop_across(near_out)
    in_gradient = core_rows([hop_out(total_a), hop_out(total_b)]) * scaling
    sum_out = hop_out(total_out)
    other_out = send(sum_out, "c", 1)
    first_out, last_out = (
        jnp.where(me_c == 0, a, b).astype(f32) * scaling
        for a, b in ((sum_out, other_out), (other_out, sum_out))
    )
    out_gradient = jnp.concatenate([first_out[:group], last_out[:group]])
    sums = pick(first_out[group : group + 6].reshape(6, columns, -1), me_f, 1)
    biases = jnp.stack([rows[group + 6 :].reshape(-1) for rows in (first_out, last_out)])
    up_bias = biases[:, :ff].reshape(CORES, planes, unit).transpose(1, 0, 2).reshape(-1)
    in_bias = biases[:, ff : ff + 2 * group].reshape(CORES, 2, group).transpose(1, 0, 2)
    in_bias = in_bias.reshape(2, -1)
    down_gradient = down_full.astype(f32) * scaling
    up_gradient = up_full.astype(f32) * scaling

    return (
        layer_output[None],
        input_gradient[None],
        sums[0],
        sums[1],
        in_gradient,
        in_bias,
        out_gradient,
        sums[2],
        sums[3],
        sums[4],
        up_gradient,
        up_bias,
        down_gradient,
        sums[5],
    )


def solution(mesh):
    columns, seq = mesh.devices.shape
    split = Mesh(mesh.devices.reshape(columns, seq // CORES, CORES), ("f", "z", "c"))
    rows = P("f", ("z", "c"), None)
    vector, matrix, paired = P("f"), P("f", None), P(None, "f")
    return jax.shard_map(
        local,
        mesh=split,
        in_specs=(
            rows,
            P("f", None),
            rows,
            vector,
            vector,
            matrix,
            paired,
            matrix,
            vector,
            vector,
            vector,
            matrix,
            vector,
            matrix,
            vector,
        ),
        out_specs=(
            rows,
            rows,
            vector,
            vector,
            matrix,
            paired,
            matrix,
            vector,
            vector,
            vector,
            matrix,
            vector,
            matrix,
            vector,
        ),
        check_vma=False,
    )
```

```python
import functools

import jax
import jax.numpy as jnp
from jax import lax
from jax.experimental import pallas as pl
from jax.experimental.pallas import tpu as pltpu
from jax.sharding import Mesh, PartitionSpec as P

HEADS = 32
HEAD_DIM = 64
BLOCK = 128
DOCS = 4
TILE = 256
CORES = 2
MASKED = -1e30

epsilon = 1e-05
bf16 = jnp.bfloat16
f32 = jnp.float32


def contract(a, b, da, db):
    return lax.dot_general(a, b, (((da,), (db,)), ((), ())), preferred_element_type=f32)


def tile_bias(bias_ref, slope_ref, pair):
    keys = lax.broadcasted_iota(jnp.int32, (TILE, TILE), 0)
    queries = lax.broadcasted_iota(jnp.int32, (TILE, TILE), 1)
    gap = (keys - queries).astype(f32)
    for h in range(2):
        bias_ref[h] = gap * slope_ref[pair * 2 + h]


def head_halves(block):
    lane = lax.broadcasted_iota(jnp.int32, block.shape, 1)
    zero = jnp.zeros_like(block)
    return [jnp.where((lane // HEAD_DIM) == h, block, zero) for h in range(2)]


def forward_kernel(
    first_ref, slope_ref, q_ref, k_ref, v_ref, low_ref, high_ref, out_ref, lse_ref, vt_ref, bias_ref
):
    pair, qi = pl.program_id(0), pl.program_id(1)

    @pl.when(qi == 0)
    def _():
        vt_ref[...] = v_ref[...].T
        tile_bias(bias_ref, slope_ref, pair)

    queries = head_halves(q_ref[...] * jnp.asarray(HEAD_DIM**-0.5, bf16))
    low, high = low_ref[...], high_ref[...]
    rows = lax.broadcasted_iota(jnp.int32, (TILE, TILE), 0)
    here = pl.multiple_of(qi * TILE, TILE)
    diagonal = k_ref[pl.ds(here, TILE), :]
    inside = (rows >= low - here) & (rows < high - here)
    state = []
    for h in range(2):
        scores = contract(diagonal, queries[h], 1, 1) - jnp.abs(bias_ref[h])
        scores = jnp.where(inside, scores, MASKED)
        peak = jnp.max(scores, axis=0, keepdims=True)
        weights = jnp.exp(scores - peak)
        total = jnp.sum(weights, axis=0, keepdims=True)
        values = vt_ref[pl.ds(h * HEAD_DIM, HEAD_DIM), pl.ds(here, TILE)]
        state += [peak, total, contract(values, weights.astype(bf16), 1, 0)]

    def step(t, state):
        start = pl.multiple_of(t * TILE, TILE)
        keys = k_ref[pl.ds(start, TILE), :]
        seen = rows >= low - start
        away = ((t - qi) * TILE).astype(f32)
        fresh = []
        for h in range(2):
            peak, total, mixed = state[3 * h : 3 * h + 3]
            scores = contract(keys, queries[h], 1, 1) + bias_ref[h]
            scores = jnp.where(seen, scores, MASKED)
            offset = away * slope_ref[pair * 2 + h]
            top = jnp.maximum(peak, jnp.max(scores, axis=0, keepdims=True) + offset)
            weights = jnp.exp(scores + (offset - top))
            shrink = jnp.exp(peak - top)
            values = vt_ref[pl.ds(h * HEAD_DIM, HEAD_DIM), pl.ds(start, TILE)]
            fresh += [
                top,
                total * shrink + jnp.sum(weights, axis=0, keepdims=True),
                mixed * shrink + contract(values, weights.astype(bf16), 1, 0),
            ]
        return tuple(fresh)

    state = lax.fori_loop(first_ref[qi], qi, step, tuple(state))
    mixed = jnp.concatenate([state[2] / state[1], state[5] / state[4]], axis=0)
    out_ref[...] = mixed.T.astype(bf16)
    lse_ref[0] = jnp.concatenate([state[0] + jnp.log(state[1]), state[3] + jnp.log(state[4])], axis=0)


def backward_kernel(
    first_ref,
    slope_ref,
    q_ref,
    k_ref,
    v_ref,
    out_ref,
    grad_ref,
    lse_ref,
    low_ref,
    high_ref,
    dq_ref,
    dk_ref,
    dv_ref,
    kt_ref,
    bias_ref,
    dk_sum,
    dv_sum,
    dq_sum,
):
    pair, qi = pl.program_id(0), pl.program_id(1)

    @pl.when(qi == 0)
    def _():
        kt_ref[...] = k_ref[...].T
        tile_bias(bias_ref, slope_ref, pair)
        dk_sum[...] = jnp.zeros_like(dk_sum)
        dv_sum[...] = jnp.zeros_like(dv_sum)

    queries = head_halves(q_ref[...] * jnp.asarray(HEAD_DIM**-0.5, bf16))
    grads = head_halves(grad_ref[...])
    low, high = low_ref[...], high_ref[...]
    rows = lax.broadcasted_iota(jnp.int32, (TILE, TILE), 0)
    product = (grad_ref[...].astype(f32) * out_ref[...].astype(f32)).T
    deltas = [
        jnp.sum(product[h * HEAD_DIM : (h + 1) * HEAD_DIM], axis=0, keepdims=True) for h in range(2)
    ]
    lse = [lse_ref[0, pl.ds(h, 1), :] for h in range(2)]
    dq_sum[...] = jnp.zeros_like(dq_sum)

    def tile(start, on_diagonal, offsets):
        keys = k_ref[pl.ds(start, TILE), :]
        values = v_ref[pl.ds(start, TILE), :]
        seen = rows >= low - start
        if on_diagonal:
            seen = seen & (rows < high - start)
        dk, dv = dk_sum[pl.ds(start, TILE), :], dv_sum[pl.ds(start, TILE), :]
        for h in range(2):
            scores = contract(keys, queries[h], 1, 1)
            if on_diagonal:
                scores = scores - jnp.abs(bias_ref[h]) - lse[h]
            else:
                scores = scores + bias_ref[h] + (offsets[h] - lse[h])
            probs = jnp.exp(jnp.where(seen, scores, MASKED))
            pull = contract(values, grads[h], 1, 1)
            grad_scores = (probs * (pull - deltas[h])).astype(bf16)
            dv = dv + contract(probs.astype(bf16), grads[h], 1, 0)
            dk = dk + contract(grad_scores, queries[h], 1, 0)
            keys_t = kt_ref[pl.ds(h * HEAD_DIM, HEAD_DIM), pl.ds(start, TILE)]
            dq_sum[pl.ds(h * HEAD_DIM, HEAD_DIM), :] += contract(keys_t, grad_scores, 1, 0)
        dk_sum[pl.ds(start, TILE), :] = dk
        dv_sum[pl.ds(start, TILE), :] = dv

    tile(pl.multiple_of(qi * TILE, TILE), True, None)

    def step(t, carry):
        away = ((t - qi) * TILE).astype(f32)
        tile(
            pl.multiple_of(t * TILE, TILE),
            False,
            [away * slope_ref[pair * 2 + h] for h in range(2)],
        )
        return carry

    lax.fori_loop(first_ref[qi], qi, step, 0)
    dq_ref[...] = (dq_sum[...] * HEAD_DIM**-0.5).T.astype(bf16)

    @pl.when(qi == pl.num_programs(1) - 1)
    def _():
        dk_ref[...] = dk_sum[...].astype(bf16)
        dv_ref[...] = dv_sum[...].astype(bf16)


def attention_specs(length, pairs):
    wide = 2 * HEAD_DIM

    def tiles(third):
        return pl.BlockSpec((TILE, wide), lambda p, i, *_: (i, third * pairs + p))

    def whole(third):
        return pl.BlockSpec((length, wide), lambda p, i, *_: (0, third * pairs + p))

    limits = pl.BlockSpec((1, TILE), lambda p, i, *_: (0, i))
    lse = pl.BlockSpec((1, 2, TILE), lambda p, i, *_: (p, 0, i))
    return tiles, whole, limits, lse


def attention(stacked, low, high, first, slopes):
    length, pairs = stacked.shape[0], stacked.shape[1] // (6 * HEAD_DIM)
    tiles, whole, limits, lse = attention_specs(length, pairs)
    return pl.pallas_call(
        forward_kernel,
        grid_spec=pltpu.PrefetchScalarGridSpec(
            num_scalar_prefetch=2,
            grid=(pairs, length // TILE),
            in_specs=[tiles(0), whole(1), whole(2), limits, limits],
            out_specs=[tiles(0), lse],
            scratch_shapes=[
                pltpu.VMEM((2 * HEAD_DIM, length), bf16),
                pltpu.VMEM((2, TILE, TILE), f32),
            ],
        ),
        out_shape=[
            jax.ShapeDtypeStruct((length, pairs * 2 * HEAD_DIM), bf16),
            jax.ShapeDtypeStruct((pairs, 2, length), f32),
        ],
        compiler_params=pltpu.CompilerParams(vmem_limit_bytes=32 << 20),
        cost_estimate=pl.CostEstimate(
            flops=30_000_000_000, bytes_accessed=4 << 20, transcendentals=1 << 20
        ),
        name="attention_forward",
    )(first, slopes, stacked, stacked, stacked, low, high)


def attention_back(stacked, mixed, grads, lse_rows, low, high, first, slopes):
    length, pairs = stacked.shape[0], stacked.shape[1] // (6 * HEAD_DIM)
    tiles, whole, limits, lse = attention_specs(length, pairs)
    shape = jax.ShapeDtypeStruct((length, pairs * 2 * HEAD_DIM), bf16)
    return pl.pallas_call(
        backward_kernel,
        grid_spec=pltpu.PrefetchScalarGridSpec(
            num_scalar_prefetch=2,
            grid=(pairs, length // TILE),
            in_specs=[tiles(0), whole(1), whole(2), tiles(0), tiles(0), lse, limits, limits],
            out_specs=[tiles(0), whole(0), whole(0)],
            scratch_shapes=[
                pltpu.VMEM((2 * HEAD_DIM, length), bf16),
                pltpu.VMEM((2, TILE, TILE), f32),
                pltpu.VMEM((length, 2 * HEAD_DIM), f32),
                pltpu.VMEM((length, 2 * HEAD_DIM), f32),
                pltpu.VMEM((2 * HEAD_DIM, TILE), f32),
            ],
        ),
        out_shape=[shape, shape, shape],
        compiler_params=pltpu.CompilerParams(vmem_limit_bytes=32 << 20),
        cost_estimate=pl.CostEstimate(
            flops=30_000_000_000, bytes_accessed=8 << 20, transcendentals=1 << 20
        ),
        name="attention_backward",
    )(first, slopes, stacked, stacked, stacked, mixed, grads, lse_rows, low, high)


def moments(values):
    centre = jnp.mean(values, axis=-1, keepdims=True)
    offset = values - centre
    rate = lax.rsqrt(jnp.mean(offset * offset, axis=-1, keepdims=True) + epsilon)
    return offset * rate, rate


def norm_back(grads, unit, rate, gain):
    scaled = grads * gain
    mean = jnp.mean(scaled, axis=-1, keepdims=True)
    along = jnp.mean(scaled * unit, axis=-1, keepdims=True)
    return rate * (scaled - mean - unit * along)


def dot(a, b):
    return jnp.dot(a, b, preferred_element_type=f32)


def gelu_parts(values):
    phi = 0.5 * (1.0 + lax.erf(values * (0.5**0.5)))
    density = jnp.exp(-0.5 * values * values) * 0.3989422804014327
    return values * phi, phi + values * density


def pick(values, index, axis):
    return lax.dynamic_index_in_dim(values, index, axis, keepdims=False)


def put(values, piece, *index):
    return lax.dynamic_update_slice(values, piece, index)


def send(values, axis, distance):
    n = lax.axis_size(axis)
    return lax.ppermute(values, axis, [(i, i ^ distance) for i in range(n)])


def butterfly(values, axes):
    for axis in axes:
        distance = 1
        while distance < lax.axis_size(axis):
            values = values + send(values, axis, distance)
            distance *= 2
    return values


def tie(values, *others):
    for other in others:
        first = lax.slice(other, (0,) * other.ndim, (1,) * other.ndim).reshape(())
        values = values + (first.astype(f32) * 0.0).astype(values.dtype)
    return values


def exchange(values, axis):
    return lax.all_to_all(values, axis, split_axis=0, concat_axis=0, tiled=True)


def to_planes(rows):
    split = rows.reshape((lax.axis_size("f"), -1) + rows.shape[1:])
    return exchange(exchange(split, "f"), "z")


def from_planes(blocks):
    rows = exchange(exchange(blocks, "z"), "f")
    return rows.reshape((-1,) + blocks.shape[2:])


def by_position(values, blocks):
    split = values.reshape(lax.axis_size("f"), CORES, blocks, -1, values.shape[-1])
    return split.transpose(2, 1, 0, 3, 4).reshape(values.shape)


def by_owner(values, blocks):
    split = values.reshape(blocks, CORES, lax.axis_size("f"), -1, values.shape[-1])
    return split.transpose(2, 1, 0, 3, 4).reshape(values.shape)


def core_gather(own):
    n = lax.axis_size("f")
    half = own.shape[0] // 2
    if n != 4:
        return jnp.concatenate([own] + [send(own, "f", d) for d in range(1, n)])
    along_x, along_y = send(own, "f", 1), send(own, "f", 2)
    far = [send(along_x[:half], "f", 2), send(along_y[half:], "f", 1)]
    return jnp.concatenate([own, along_x, along_y] + far)


def plane_scatter(partial, *floor):
    n = lax.axis_size("f")
    me_f, me_c = lax.axis_index("f"), lax.axis_index("c")
    split = partial.reshape(n, CORES, -1, partial.shape[-1])
    half = split.shape[2] // 2
    other = send(tie(pick(split, 1 - me_c, 1), *floor), "c", 1)
    near = (pick(split, me_c, 1).astype(f32) + other.astype(f32)).astype(bf16)

    def block(distance):
        return pick(near, me_f ^ distance, 0)

    if n == 4:
        far = block(3)
        for_y, for_x = send(far[:half], "f", 1), send(far[half:], "f", 2)
        near_x, near_y = block(1), block(2)
        near_x = jnp.concatenate([near_x[:half], near_x[half:] + for_x])
        near_y = jnp.concatenate([near_y[:half] + for_y, near_y[half:]])
        from_x, from_y = send(near_x, "f", 1), send(near_y, "f", 2)
        return block(0).astype(f32) + from_x.astype(f32) + from_y.astype(f32)
    total = block(0).astype(f32)
    for d in range(1, n):
        total = total + send(block(d), "f", d).astype(f32)
    return total


def heads_to_tokens(mixed):
    devices = lax.axis_size("f") * CORES
    parts = exchange(mixed.reshape(devices, -1, mixed.shape[-1]), ("f", "c"))
    return parts.transpose(1, 0, 2).reshape(parts.shape[1], -1)


def tokens_to_heads(rows):
    devices = lax.axis_size("f") * CORES
    parts = rows.reshape(rows.shape[0], devices, -1).transpose(1, 0, 2)
    return exchange(parts, ("f", "c")).reshape(-1, parts.shape[-1])


def local(
    inputs,
    documents,
    cotangent,
    attend_gain,
    attend_shift,
    project_in,
    project_bias,
    project_out,
    output_bias,
    feed_gain,
    feed_shift,
    expand_weight,
    expand_bias,
    reduce_weight,
    reduce_bias,
):
    columns, planes = lax.axis_size("f"), lax.axis_size("z")
    me_f, me_z, me_c = lax.axis_index("f"), lax.axis_index("z"), lax.axis_index("c")
    width = inputs.shape[2]
    length = documents.shape[1]
    hidden = expand_weight.shape[1]
    device_heads = HEADS // (columns * CORES)
    group = device_heads * HEAD_DIM
    ff = hidden // (columns * CORES)
    unit = ff // planes
    scaling = (columns * length) ** (-0.5)

    vectors = jnp.stack([attend_gain, attend_shift, output_bias, feed_gain, feed_shift, reduce_bias])
    vectors = lax.all_gather(vectors, "f", axis=1, tiled=True).astype(f32)
    gain_one, shift_one, bias_out, gain_two, shift_two, bias_reduce = vectors

    split = tie(inputs[0], vectors).reshape(columns, -1, width)
    split = exchange(split, "f")
    tokens = exchange(split, "z").reshape(-1, width)
    turn = [(a * planes + b, b * planes + a) for a in range(columns) for b in range(planes)]
    docs = lax.ppermute(documents, ("f", "z"), turn)

    deep = project_in.shape[0]
    weight_in = jnp.zeros((width, 3 * group), bf16)
    for d in range(columns):
        column = ((me_f ^ d) * CORES + me_c) * group
        piece = jnp.concatenate(
            [
                lax.dynamic_slice(project_in, (0, third * width + column), (deep, group))
                for third in range(3)
            ],
            axis=1,
        )
        piece = send(piece, "f", d) if d else piece
        weight_in = put(weight_in, piece, (me_f ^ d) * deep, 0)
    grad_own = to_planes(tie(cotangent[0], tokens)).reshape(-1, width)
    strip = expand_weight.shape[0] // planes
    strips = lax.dynamic_slice_in_dim(expand_weight, me_z * strip, strip)
    turned = jnp.stack(
        [
            jnp.concatenate(
                [
                    lax.dynamic_slice(
                        strips, (0, (j * planes + p) * CORES * unit + me_c * unit), (strip, unit)
                    )
                    for p in range(planes)
                ],
                axis=1,
            )
            for j in range(columns)
        ]
    )
    turned = exchange(tie(turned, tokens), "f")
    up_pieces = [send(turned, "z", e) if e else turned for e in range(planes)]
    weight_down = pick(reduce_weight.reshape(planes, CORES, unit, width), me_c, 1).reshape(ff, width)
    bias_pair = pick(project_bias.reshape(2, CORES, group), me_c, 1).astype(f32)
    bias_in = jnp.concatenate([bias_pair[0], jnp.zeros((group,), f32), bias_pair[1]])
    bias_up = pick(expand_bias.reshape(planes, CORES, unit), me_c, 1).reshape(ff).astype(f32)

    doc_row = docs[0]
    position = jnp.arange(length, dtype=jnp.int32)
    low = jnp.zeros_like(doc_row)
    end = jnp.zeros_like(doc_row)
    for d in range(DOCS):
        low = jnp.where(doc_row == d, jnp.sum((doc_row < d).astype(jnp.int32)), low)
        end = jnp.where(doc_row == d, jnp.sum((doc_row <= d).astype(jnp.int32)), end)
    high = jnp.minimum(end, (position // BLOCK + 1) * BLOCK)
    first = low[::TILE] // TILE
    low, high = low[None], high[None]
    first_head = (me_f * CORES + me_c) * device_heads
    heads = first_head + 1 + jnp.arange(device_heads, dtype=jnp.int32)
    slopes = 2.0 ** (-8.0 * heads.astype(f32) / HEADS)

    token_rows = tie(tokens.astype(f32), weight_in)
    unit_one, rate_one = moments(token_rows)
    normed_one = (unit_one * gain_one + shift_one).astype(bf16)
    normed_one = lax.all_gather(normed_one, ("f", "c"), axis=0, tiled=True)
    stacked = tie(dot(normed_one, weight_in) + bias_in, grad_own, turned)
    stacked = by_position(stacked.astype(bf16), planes)
    mine = tie(pick(project_out.reshape(CORES, -1, width), me_c, 0), stacked)
    weight_out = lax.all_gather(mine, ("f", "c"), axis=0, tiled=True)
    mixed, lse_rows = attention(stacked, low, high, first, slopes)
    mixed_owned = by_owner(mixed, planes)
    weight_up = jnp.zeros((columns, planes, strip, ff), bf16)
    for e in range(planes):
        piece = up_pieces[e][:, None]
        weight_up = put(weight_up, piece, 0, me_z ^ e, 0, 0)
    weight_up = weight_up.reshape(width, ff)
    middle = token_rows + (dot(heads_to_tokens(mixed_owned), weight_out) + bias_out)
    unit_two, rate_two = moments(middle)
    grad_all = lax.all_gather(tie(grad_own, mixed), ("f", "c"), axis=0, tiled=True)
    normed_two = (unit_two * gain_two + shift_two).astype(bf16)
    normed_two = lax.all_gather(normed_two, ("f", "c"), axis=0, tiled=True)
    hidden_pre = dot(normed_two, weight_up) + bias_up
    active, slope = gelu_parts(hidden_pre)
    active = active.astype(bf16)

    down_term = contract(active, grad_all, 0, 0).astype(bf16)
    grad_active = tie(contract(grad_all, weight_down, 1, 1), down_term)
    grad_hidden = (grad_active * slope).astype(bf16)
    grad_partial = contract(grad_hidden, weight_up, 1, 1).astype(bf16)
    up_term = tie(contract(normed_two, grad_hidden, 0, 0), grad_partial).astype(bf16)
    forward_partial = tie(dot(active, weight_down), up_term).astype(bf16)
    down_share = lax.psum_scatter(down_term, "z", scatter_dimension=0, tiled=True)
    grad_two = tie(plane_scatter(grad_partial), up_term, forward_partial)
    up_share = up_term.reshape(columns, -1, ff)
    up_share = lax.psum_scatter(up_share, "z", scatter_dimension=1, tiled=True)

    grad_rows = grad_own.astype(f32)
    grad_middle = grad_rows + norm_back(grad_two, unit_two, rate_two, gain_two)
    grad_branch = grad_middle.astype(bf16)
    grad_mixed_owned = tokens_to_heads(contract(grad_branch, weight_out, 1, 1).astype(bf16))
    grad_mixed = tie(by_position(grad_mixed_owned, planes), down_share)
    branch_mine = core_gather(tie(grad_branch, grad_mixed_owned))
    branch_other = send(branch_mine, "c", 1)
    layer_sum = plane_scatter(forward_partial, grad_mixed_owned)
    dq, dk, dv = attention_back(stacked, mixed, grad_mixed, lse_rows, low, high, first, slopes)
    grad_projected = by_owner(jnp.concatenate([dq, dk, dv], axis=1), planes)
    grad_partial = contract(grad_projected, weight_in, 1, 1).astype(bf16)
    in_term = tie(contract(normed_one, grad_projected, 0, 0), grad_partial, up_share).astype(bf16)
    down_full = lax.all_gather(tie(down_share, dq), ("z", "c"), axis=0, tiled=True)
    grad_one = tie(plane_scatter(grad_partial), in_term)

    up_rows = tie(up_share, grad_one).reshape(columns * CORES, -1, ff)
    up_rows = exchange(up_rows, ("f", "c")).reshape(columns, CORES, -1, planes, unit)
    up_rows = up_rows.transpose(2, 0, 3, 1, 4).reshape(-1, hidden)
    in_share = in_term.reshape(columns, -1, 3 * group)
    in_share = lax.psum_scatter(in_share, "z", scatter_dimension=1, tiled=True)
    up_full = lax.all_gather(up_rows, ("z", "c"), axis=0, tiled=True)
    in_rows = exchange(in_share.reshape(columns * CORES, -1, 3 * group), ("f", "c"))
    in_rows = in_rows.reshape(columns * CORES, -1, 3, group).transpose(1, 2, 0, 3)
    in_rows = in_rows.reshape(-1, 3 * width)
    in_full = lax.all_gather(in_rows, ("z", "c"), axis=0, tiled=True)
    input_rows = grad_middle + norm_back(grad_one, unit_one, rate_one, gain_one)
    input_rows = tie(input_rows, up_rows, down_full)
    input_gradient = from_planes(input_rows.astype(bf16).reshape(planes, -1, width))
    mixed_cores = mixed_owned.reshape(columns, CORES, -1, group)

    def near_rows(core):
        rows = []
        for d in range(columns):
            size = (1, 1) + mixed_cores.shape[2:]
            rows.append(lax.dynamic_slice(mixed_cores, (me_f ^ d, core, 0, 0), size))
        return jnp.concatenate(rows).reshape(-1, group)

    out_term = contract(near_rows(me_c), branch_mine, 0, 0)
    out_term = (out_term + contract(near_rows(1 - me_c), branch_other, 0, 0)).astype(bf16)

    sums = jnp.stack(
        [
            jnp.sum(grad_one * unit_one, axis=0),
            jnp.sum(grad_one, axis=0),
            jnp.sum(grad_branch.astype(f32), axis=0),
            jnp.sum(grad_two * unit_two, axis=0),
            jnp.sum(grad_two, axis=0),
            jnp.sum(grad_rows, axis=0),
        ]
    )
    sums = butterfly(sums, ("c", "f"))
    biases = jnp.concatenate(
        [
            jnp.sum(grad_hidden.astype(f32), axis=0),
            jnp.sum(dq.astype(f32), axis=0),
            jnp.sum(dv.astype(f32), axis=0),
        ]
    )
    biases = jnp.pad(biases, (0, (16 * planes - 6) * width - biases.shape[0])).reshape(-1, width)
    out_term = jnp.concatenate([out_term, sums.astype(bf16), biases.astype(bf16)])
    out_share = exchange(out_term.reshape(planes, -1, width), "z").astype(f32)
    out_share = jnp.sum(out_share, axis=0).astype(bf16)
    out_full = lax.all_gather(out_share, ("z", "c"), axis=0, tiled=False)

    layer_rows = tie(middle + layer_sum + bias_reduce, input_gradient).astype(bf16)
    layer_output = from_planes(layer_rows.reshape(planes, -1, width))
    input_gradient = input_gradient.astype(f32)

    out_full = out_full.reshape(planes, CORES, -1, width).transpose(1, 0, 2, 3)
    first_out, last_out = out_full.reshape(CORES, -1, width).astype(f32) * scaling
    out_gradient = jnp.concatenate([first_out[:group], last_out[:group]])
    sums = pick(first_out[group : group + 6].reshape(6, columns, -1), me_f, 1)
    biases = jnp.stack([rows[group + 6 :].reshape(-1) for rows in (first_out, last_out)])
    up_bias = biases[:, :ff].reshape(CORES, planes, unit).transpose(1, 0, 2).reshape(-1)
    in_bias = biases[:, ff : ff + 2 * group].reshape(CORES, 2, group).transpose(1, 0, 2)
    in_bias = in_bias.reshape(2, -1)
    in_gradient = in_full.astype(f32) * scaling
    down_gradient = down_full.astype(f32) * scaling
    up_gradient = up_full.astype(f32) * scaling

    return (
        layer_output[None],
        input_gradient[None],
        sums[0],
        sums[1],
        in_gradient,
        in_bias,
        out_gradient,
        sums[2],
        sums[3],
        sums[4],
        up_gradient,
        up_bias,
        down_gradient,
        sums[5],
    )


def solution(mesh):
    columns, seq = mesh.devices.shape
    split = Mesh(mesh.devices.reshape(columns, seq // CORES, CORES), ("f", "z", "c"))
    rows = P("f", ("z", "c"), None)
    vector, matrix, paired = P("f"), P("f", None), P(None, "f")
    return jax.shard_map(
        local,
        mesh=split,
        in_specs=(
            rows,
            P("f", None),
            rows,
            vector,
            vector,
            matrix,
            paired,
            matrix,
            vector,
            vector,
            vector,
            matrix,
            vector,
            matrix,
            vector,
        ),
        out_specs=(
            rows,
            rows,
            vector,
            vector,
            matrix,
            paired,
            matrix,
            vector,
            vector,
            vector,
            matrix,
            vector,
            matrix,
            vector,
        ),
        check_vma=False,
    )
```

```python
import functools

import jax
import jax.numpy as jnp
from jax import lax
from jax.experimental import pallas as pl
from jax.experimental.pallas import tpu as pltpu
from jax.sharding import Mesh, PartitionSpec as P

HEADS = 32
HEAD_DIM = 64
BLOCK = 128
DOCS = 4
TILE = 256
CORES = 2
MASKED = -1e30

epsilon = 1e-05
bf16 = jnp.bfloat16
f32 = jnp.float32


def contract(a, b, da, db):
    return lax.dot_general(a, b, (((da,), (db,)), ((), ())), preferred_element_type=f32)


def tile_bias(bias_ref, slope_ref, pair):
    keys = lax.broadcasted_iota(jnp.int32, (TILE, TILE), 0)
    queries = lax.broadcasted_iota(jnp.int32, (TILE, TILE), 1)
    gap = (keys - queries).astype(f32)
    for h in range(2):
        bias_ref[h] = gap * slope_ref[pair * 2 + h]


def head_halves(block):
    lane = lax.broadcasted_iota(jnp.int32, block.shape, 1)
    zero = jnp.zeros_like(block)
    return [jnp.where((lane // HEAD_DIM) == h, block, zero) for h in range(2)]


def forward_kernel(
    first_ref, slope_ref, q_ref, k_ref, v_ref, low_ref, high_ref, out_ref, lse_ref, vt_ref, bias_ref
):
    qi = pl.program_id(0)
    wide = 2 * HEAD_DIM
    pairs = q_ref.shape[1] // wide
    heads = range(2 * pairs)

    @pl.when(qi == 0)
    def _():
        vt_ref[...] = v_ref[...].T
        for pair in range(pairs):
            tile_bias(bias_ref.at[pl.ds(2 * pair, 2)], slope_ref, pair)

    scale = jnp.asarray(HEAD_DIM**-0.5, bf16)
    queries = []
    for pair in range(pairs):
        queries += head_halves(q_ref[:, pl.ds(pair * wide, wide)] * scale)
    low, high = low_ref[...], high_ref[...]
    rows = lax.broadcasted_iota(jnp.int32, (TILE, TILE), 0)

    def scores_of(h, start):
        keys = k_ref[pl.ds(start, TILE), pl.ds(h // 2 * wide, wide)]
        return contract(keys, queries[h], 1, 1)

    def mix(h, start, weights):
        values = vt_ref[pl.ds(h * HEAD_DIM, HEAD_DIM), pl.ds(start, TILE)]
        return contract(values, weights.astype(bf16), 1, 0)

    here = pl.multiple_of(qi * TILE, TILE)
    inside = (rows >= low - here) & (rows < high - here)
    state = []
    for h in heads:
        scores = jnp.where(inside, scores_of(h, here) - jnp.abs(bias_ref[h]), MASKED)
        peak = jnp.max(scores, axis=0, keepdims=True)
        weights = jnp.exp(scores - peak)
        state += [peak, jnp.sum(weights, axis=0, keepdims=True), mix(h, here, weights)]

    def step(t, state):
        start = pl.multiple_of(t * TILE, TILE)
        seen = rows >= low - start
        away = ((t - qi) * TILE).astype(f32)
        fresh = []
        for h in heads:
            peak, total, mixed = state[3 * h : 3 * h + 3]
            scores = jnp.where(seen, scores_of(h, start) + bias_ref[h], MASKED)
            offset = away * slope_ref[h]
            top = jnp.maximum(peak, jnp.max(scores, axis=0, keepdims=True) + offset)
            weights = jnp.exp(scores + (offset - top))
            shrink = jnp.exp(peak - top)
            total = total * shrink + jnp.sum(weights, axis=0, keepdims=True)
            fresh += [top, total, mixed * shrink + mix(h, start, weights)]
        return tuple(fresh)

    state = lax.fori_loop(first_ref[qi], qi, step, tuple(state))
    for pair in range(pairs):
        sides = [state[3 * h + 2] / state[3 * h + 1] for h in (2 * pair, 2 * pair + 1)]
        out_ref[:, pl.ds(pair * wide, wide)] = jnp.concatenate(sides, axis=0).T.astype(bf16)
        sides = [state[3 * h] + jnp.log(state[3 * h + 1]) for h in (2 * pair, 2 * pair + 1)]
        lse_ref[pair] = jnp.concatenate(sides, axis=0)


def backward_kernel(
    first_ref,
    slope_ref,
    q_ref,
    k_ref,
    v_ref,
    out_ref,
    grad_ref,
    lse_ref,
    low_ref,
    high_ref,
    dq_ref,
    dk_ref,
    dv_ref,
    kt_ref,
    bias_ref,
    dk_sum,
    dv_sum,
    dq_sum,
):
    pair, qi = pl.program_id(0), pl.program_id(1)

    @pl.when(qi == 0)
    def _():
        kt_ref[...] = k_ref[...].T
        tile_bias(bias_ref, slope_ref, pair)
        dk_sum[...] = jnp.zeros_like(dk_sum)
        dv_sum[...] = jnp.zeros_like(dv_sum)

    queries = head_halves(q_ref[...] * jnp.asarray(HEAD_DIM**-0.5, bf16))
    grads = head_halves(grad_ref[...])
    low, high = low_ref[...], high_ref[...]
    rows = lax.broadcasted_iota(jnp.int32, (TILE, TILE), 0)
    product = (grad_ref[...].astype(f32) * out_ref[...].astype(f32)).T
    deltas = [
        jnp.sum(product[h * HEAD_DIM : (h + 1) * HEAD_DIM], axis=0, keepdims=True) for h in range(2)
    ]
    lse = [lse_ref[0, pl.ds(h, 1), :] for h in range(2)]
    dq_sum[...] = jnp.zeros_like(dq_sum)

    def tile(start, on_diagonal, offsets):
        keys = k_ref[pl.ds(start, TILE), :]
        values = v_ref[pl.ds(start, TILE), :]
        seen = rows >= low - start
        if on_diagonal:
            seen = seen & (rows < high - start)
        dk, dv = dk_sum[pl.ds(start, TILE), :], dv_sum[pl.ds(start, TILE), :]
        for h in range(2):
            scores = contract(keys, queries[h], 1, 1)
            if on_diagonal:
                scores = scores - jnp.abs(bias_ref[h]) - lse[h]
            else:
                scores = scores + bias_ref[h] + (offsets[h] - lse[h])
            probs = jnp.exp(jnp.where(seen, scores, MASKED))
            pull = contract(values, grads[h], 1, 1)
            grad_scores = (probs * (pull - deltas[h])).astype(bf16)
            dv = dv + contract(probs.astype(bf16), grads[h], 1, 0)
            dk = dk + contract(grad_scores, queries[h], 1, 0)
            keys_t = kt_ref[pl.ds(h * HEAD_DIM, HEAD_DIM), pl.ds(start, TILE)]
            dq_sum[pl.ds(h * HEAD_DIM, HEAD_DIM), :] += contract(keys_t, grad_scores, 1, 0)
        dk_sum[pl.ds(start, TILE), :] = dk
        dv_sum[pl.ds(start, TILE), :] = dv

    tile(pl.multiple_of(qi * TILE, TILE), True, None)

    def step(t, carry):
        away = ((t - qi) * TILE).astype(f32)
        tile(
            pl.multiple_of(t * TILE, TILE),
            False,
            [away * slope_ref[pair * 2 + h] for h in range(2)],
        )
        return carry

    lax.fori_loop(first_ref[qi], qi, step, 0)
    dq_ref[...] = (dq_sum[...] * HEAD_DIM**-0.5).T.astype(bf16)

    @pl.when(qi == pl.num_programs(1) - 1)
    def _():
        dk_ref[...] = dk_sum[...].astype(bf16)
        dv_ref[...] = dv_sum[...].astype(bf16)


def attention_specs(length, pairs):
    wide = 2 * HEAD_DIM

    def tiles(third):
        return pl.BlockSpec((TILE, wide), lambda p, i, *_: (i, third * pairs + p))

    def whole(third):
        return pl.BlockSpec((length, wide), lambda p, i, *_: (0, third * pairs + p))

    limits = pl.BlockSpec((1, TILE), lambda p, i, *_: (0, i))
    lse = pl.BlockSpec((1, 2, TILE), lambda p, i, *_: (p, 0, i))
    return tiles, whole, limits, lse


def attention(stacked, low, high, first, slopes):
    length, pairs = stacked.shape[0], stacked.shape[1] // (6 * HEAD_DIM)
    width = pairs * 2 * HEAD_DIM
    limits = pl.BlockSpec((1, TILE), lambda i, *_: (0, i))
    return pl.pallas_call(
        forward_kernel,
        grid_spec=pltpu.PrefetchScalarGridSpec(
            num_scalar_prefetch=2,
            grid=(length // TILE,),
            in_specs=[
                pl.BlockSpec((TILE, width), lambda i, *_: (i, 0)),
                pl.BlockSpec((length, width), lambda i, *_: (0, 1)),
                pl.BlockSpec((length, width), lambda i, *_: (0, 2)),
                limits,
                limits,
            ],
            out_specs=[
                pl.BlockSpec((TILE, width), lambda i, *_: (i, 0)),
                pl.BlockSpec((pairs, 2, TILE), lambda i, *_: (0, 0, i)),
            ],
            scratch_shapes=[
                pltpu.VMEM((width, length), bf16),
                pltpu.VMEM((2 * pairs, TILE, TILE), f32),
            ],
        ),
        out_shape=[
            jax.ShapeDtypeStruct((length, width), bf16),
            jax.ShapeDtypeStruct((pairs, 2, length), f32),
        ],
        compiler_params=pltpu.CompilerParams(vmem_limit_bytes=32 << 20),
        cost_estimate=pl.CostEstimate(
            flops=30_000_000_000, bytes_accessed=4 << 20, transcendentals=1 << 20
        ),
        name="attention_forward",
    )(first, slopes, stacked, stacked, stacked, low, high)


def attention_back(stacked, mixed, grads, lse_rows, low, high, first, slopes):
    length, pairs = stacked.shape[0], stacked.shape[1] // (6 * HEAD_DIM)
    tiles, whole, limits, lse = attention_specs(length, pairs)
    shape = jax.ShapeDtypeStruct((length, pairs * 2 * HEAD_DIM), bf16)
    return pl.pallas_call(
        backward_kernel,
        grid_spec=pltpu.PrefetchScalarGridSpec(
            num_scalar_prefetch=2,
            grid=(pairs, length // TILE),
            in_specs=[tiles(0), whole(1), whole(2), tiles(0), tiles(0), lse, limits, limits],
            out_specs=[tiles(0), whole(0), whole(0)],
            scratch_shapes=[
                pltpu.VMEM((2 * HEAD_DIM, length), bf16),
                pltpu.VMEM((2, TILE, TILE), f32),
                pltpu.VMEM((length, 2 * HEAD_DIM), f32),
                pltpu.VMEM((length, 2 * HEAD_DIM), f32),
                pltpu.VMEM((2 * HEAD_DIM, TILE), f32),
            ],
        ),
        out_shape=[shape, shape, shape],
        compiler_params=pltpu.CompilerParams(vmem_limit_bytes=32 << 20),
        cost_estimate=pl.CostEstimate(
            flops=30_000_000_000, bytes_accessed=8 << 20, transcendentals=1 << 20
        ),
        name="attention_backward",
    )(first, slopes, stacked, stacked, stacked, mixed, grads, lse_rows, low, high)


def moments(values):
    centre = jnp.mean(values, axis=-1, keepdims=True)
    offset = values - centre
    rate = lax.rsqrt(jnp.mean(offset * offset, axis=-1, keepdims=True) + epsilon)
    return offset * rate, rate


def norm_back(grads, unit, rate, gain):
    scaled = grads * gain
    mean = jnp.mean(scaled, axis=-1, keepdims=True)
    along = jnp.mean(scaled * unit, axis=-1, keepdims=True)
    return rate * (scaled - mean - unit * along)


def dot(a, b):
    return jnp.dot(a, b, preferred_element_type=f32)


def gelu_parts(values):
    phi = 0.5 * (1.0 + lax.erf(values * (0.5**0.5)))
    density = jnp.exp(-0.5 * values * values) * 0.3989422804014327
    return values * phi, phi + values * density


def pick(values, index, axis):
    return lax.dynamic_index_in_dim(values, index, axis, keepdims=False)


def put(values, piece, *index):
    return lax.dynamic_update_slice(values, piece, index)


def send(values, axis, distance):
    n = lax.axis_size(axis)
    return lax.ppermute(values, axis, [(i, i ^ distance) for i in range(n)])


def butterfly(values, axes):
    for axis in axes:
        distance = 1
        while distance < lax.axis_size(axis):
            values = values + send(values, axis, distance)
            distance *= 2
    return values


def tie(values, *others):
    for other in others:
        first = lax.slice(other, (0,) * other.ndim, (1,) * other.ndim).reshape(())
        values = values + (first.astype(f32) * 0.0).astype(values.dtype)
    return values


def exchange(values, axis):
    return lax.all_to_all(values, axis, split_axis=0, concat_axis=0, tiled=True)


def to_planes(rows):
    split = rows.reshape((lax.axis_size("f"), -1) + rows.shape[1:])
    return exchange(exchange(split, "f"), "z")


def from_planes(blocks):
    rows = exchange(exchange(blocks, "z"), "f")
    return rows.reshape((-1,) + blocks.shape[2:])


def by_position(values, blocks):
    split = values.reshape(lax.axis_size("f"), CORES, blocks, -1, values.shape[-1])
    return split.transpose(2, 1, 0, 3, 4).reshape(values.shape)


def by_owner(values, blocks):
    split = values.reshape(blocks, CORES, lax.axis_size("f"), -1, values.shape[-1])
    return split.transpose(2, 1, 0, 3, 4).reshape(values.shape)


def core_gather(own):
    n = lax.axis_size("f")
    half = own.shape[0] // 2
    if n != 4:
        return jnp.concatenate([own] + [send(own, "f", d) for d in range(1, n)])
    along_x, along_y = send(own, "f", 1), send(own, "f", 2)
    far = [send(along_x[:half], "f", 2), send(along_y[half:], "f", 1)]
    return jnp.concatenate([own, along_x, along_y] + far)


def plane_scatter(partial, *floor):
    n = lax.axis_size("f")
    me_f, me_c = lax.axis_index("f"), lax.axis_index("c")
    split = partial.reshape(n, CORES, -1, partial.shape[-1])
    half = split.shape[2] // 2
    other = send(tie(pick(split, 1 - me_c, 1), *floor), "c", 1)
    near = (pick(split, me_c, 1).astype(f32) + other.astype(f32)).astype(bf16)

    def block(distance):
        return pick(near, me_f ^ distance, 0)

    if n == 4:
        far = block(3)
        for_y, for_x = send(far[:half], "f", 1), send(far[half:], "f", 2)
        near_x, near_y = block(1), block(2)
        near_x = jnp.concatenate([near_x[:half], near_x[half:] + for_x])
        near_y = jnp.concatenate([near_y[:half] + for_y, near_y[half:]])
        from_x, from_y = send(near_x, "f", 1), send(near_y, "f", 2)
        return block(0).astype(f32) + from_x.astype(f32) + from_y.astype(f32)
    total = block(0).astype(f32)
    for d in range(1, n):
        total = total + send(block(d), "f", d).astype(f32)
    return total


def heads_to_tokens(mixed):
    devices = lax.axis_size("f") * CORES
    parts = exchange(mixed.reshape(devices, -1, mixed.shape[-1]), ("f", "c"))
    return parts.transpose(1, 0, 2).reshape(parts.shape[1], -1)


def tokens_to_heads(rows):
    devices = lax.axis_size("f") * CORES
    parts = rows.reshape(rows.shape[0], devices, -1).transpose(1, 0, 2)
    return exchange(parts, ("f", "c")).reshape(-1, parts.shape[-1])


def local(
    inputs,
    documents,
    cotangent,
    attend_gain,
    attend_shift,
    project_in,
    project_bias,
    project_out,
    output_bias,
    feed_gain,
    feed_shift,
    expand_weight,
    expand_bias,
    reduce_weight,
    reduce_bias,
):
    columns, planes = lax.axis_size("f"), lax.axis_size("z")
    me_f, me_z, me_c = lax.axis_index("f"), lax.axis_index("z"), lax.axis_index("c")
    width = inputs.shape[2]
    length = documents.shape[1]
    hidden = expand_weight.shape[1]
    device_heads = HEADS // (columns * CORES)
    group = device_heads * HEAD_DIM
    ff = hidden // (columns * CORES)
    unit = ff // planes
    scaling = (columns * length) ** (-0.5)

    vectors = jnp.stack([attend_gain, attend_shift, output_bias, feed_gain, feed_shift, reduce_bias])
    vectors = lax.all_gather(vectors, "f", axis=1, tiled=True).astype(f32)
    gain_one, shift_one, bias_out, gain_two, shift_two, bias_reduce = vectors

    split = tie(inputs[0], vectors).reshape(columns, -1, width)
    split = exchange(split, "f")
    tokens = exchange(split, "z").reshape(-1, width)
    turn = [(a * planes + b, b * planes + a) for a in range(columns) for b in range(planes)]
    docs = lax.ppermute(documents, ("f", "z"), turn)

    deep = project_in.shape[0]
    weight_in = jnp.zeros((width, 3 * group), bf16)
    for d in range(columns):
        column = ((me_f ^ d) * CORES + me_c) * group
        piece = jnp.concatenate(
            [
                lax.dynamic_slice(project_in, (0, third * width + column), (deep, group))
                for third in range(3)
            ],
            axis=1,
        )
        piece = send(piece, "f", d) if d else piece
        weight_in = put(weight_in, piece, (me_f ^ d) * deep, 0)
    grad_own = to_planes(tie(cotangent[0], tokens)).reshape(-1, width)
    strip = expand_weight.shape[0] // planes
    strips = lax.dynamic_slice_in_dim(expand_weight, me_z * strip, strip)
    turned = jnp.stack(
        [
            jnp.concatenate(
                [
                    lax.dynamic_slice(
                        strips, (0, (j * planes + p) * CORES * unit + me_c * unit), (strip, unit)
                    )
                    for p in range(planes)
                ],
                axis=1,
            )
            for j in range(columns)
        ]
    )
    turned = exchange(tie(turned, tokens), "f")
    up_pieces = [send(turned, "z", e) if e else turned for e in range(planes)]
    weight_down = pick(reduce_weight.reshape(planes, CORES, unit, width), me_c, 1).reshape(ff, width)
    bias_pair = pick(project_bias.reshape(2, CORES, group), me_c, 1).astype(f32)
    bias_in = jnp.concatenate([bias_pair[0], jnp.zeros((group,), f32), bias_pair[1]])
    bias_up = pick(expand_bias.reshape(planes, CORES, unit), me_c, 1).reshape(ff).astype(f32)

    doc_row = docs[0]
    position = jnp.arange(length, dtype=jnp.int32)
    low = jnp.zeros_like(doc_row)
    end = jnp.zeros_like(doc_row)
    for d in range(DOCS):
        low = jnp.where(doc_row == d, jnp.sum((doc_row < d).astype(jnp.int32)), low)
        end = jnp.where(doc_row == d, jnp.sum((doc_row <= d).astype(jnp.int32)), end)
    high = jnp.minimum(end, (position // BLOCK + 1) * BLOCK)
    first = low[::TILE] // TILE
    low, high = low[None], high[None]
    first_head = (me_f * CORES + me_c) * device_heads
    heads = first_head + 1 + jnp.arange(device_heads, dtype=jnp.int32)
    slopes = 2.0 ** (-8.0 * heads.astype(f32) / HEADS)

    token_rows = tie(tokens.astype(f32), weight_in)
    unit_one, rate_one = moments(token_rows)
    normed_one = (unit_one * gain_one + shift_one).astype(bf16)
    normed_one = lax.all_gather(normed_one, ("f", "c"), axis=0, tiled=True)
    stacked = tie(dot(normed_one, weight_in) + bias_in, grad_own, turned)
    stacked = by_position(stacked.astype(bf16), planes)
    mine = tie(pick(project_out.reshape(CORES, -1, width), me_c, 0), stacked)
    weight_out = lax.all_gather(mine, ("f", "c"), axis=0, tiled=True)
    mixed, lse_rows = attention(stacked, low, high, first, slopes)
    mixed_owned = by_owner(mixed, planes)
    weight_up = jnp.zeros((columns, planes, strip, ff), bf16)
    for e in range(planes):
        piece = up_pieces[e][:, None]
        weight_up = put(weight_up, piece, 0, me_z ^ e, 0, 0)
    weight_up = weight_up.reshape(width, ff)
    middle = token_rows + (dot(heads_to_tokens(mixed_owned), weight_out) + bias_out)
    unit_two, rate_two = moments(middle)
    grad_all = lax.all_gather(tie(grad_own, mixed), ("f", "c"), axis=0, tiled=True)
    normed_two = (unit_two * gain_two + shift_two).astype(bf16)
    normed_two = lax.all_gather(normed_two, ("f", "c"), axis=0, tiled=True)
    hidden_pre = dot(normed_two, weight_up) + bias_up
    active, slope = gelu_parts(hidden_pre)
    active = active.astype(bf16)

    down_term = contract(active, grad_all, 0, 0).astype(bf16)
    grad_active = tie(contract(grad_all, weight_down, 1, 1), down_term)
    grad_hidden = (grad_active * slope).astype(bf16)
    grad_partial = contract(grad_hidden, weight_up, 1, 1).astype(bf16)
    up_term = tie(contract(normed_two, grad_hidden, 0, 0), grad_partial).astype(bf16)
    forward_partial = tie(dot(active, weight_down), up_term).astype(bf16)
    down_share = lax.psum_scatter(down_term, "z", scatter_dimension=0, tiled=True)
    grad_two = tie(plane_scatter(grad_partial), up_term, forward_partial)
    up_share = up_term.reshape(columns, -1, ff)
    up_share = lax.psum_scatter(up_share, "z", scatter_dimension=1, tiled=True)

    grad_rows = grad_own.astype(f32)
    grad_middle = grad_rows + norm_back(grad_two, unit_two, rate_two, gain_two)
    grad_branch = grad_middle.astype(bf16)
    grad_mixed_owned = tokens_to_heads(contract(grad_branch, weight_out, 1, 1).astype(bf16))
    grad_mixed = tie(by_position(grad_mixed_owned, planes), down_share)
    branch_mine = core_gather(tie(grad_branch, grad_mixed_owned))
    branch_other = send(branch_mine, "c", 1)
    layer_sum = plane_scatter(forward_partial, grad_mixed_owned)
    dq, dk, dv = attention_back(stacked, mixed, grad_mixed, lse_rows, low, high, first, slopes)
    grad_projected = by_owner(jnp.concatenate([dq, dk, dv], axis=1), planes)
    grad_partial = contract(grad_projected, weight_in, 1, 1).astype(bf16)
    in_term = tie(contract(normed_one, grad_projected, 0, 0), grad_partial, up_share).astype(bf16)
    down_full = lax.all_gather(tie(down_share, dq), ("z", "c"), axis=0, tiled=True)
    grad_one = tie(plane_scatter(grad_partial), in_term)

    up_rows = tie(up_share, grad_one).reshape(columns * CORES, -1, ff)
    up_rows = exchange(up_rows, ("f", "c")).reshape(columns, CORES, -1, planes, unit)
    up_rows = up_rows.transpose(2, 0, 3, 1, 4).reshape(-1, hidden)
    in_share = in_term.reshape(columns, -1, 3 * group)
    in_share = lax.psum_scatter(in_share, "z", scatter_dimension=1, tiled=True)
    up_full = lax.all_gather(up_rows, ("z", "c"), axis=0, tiled=True)
    in_rows = exchange(in_share.reshape(columns * CORES, -1, 3 * group), ("f", "c"))
    in_rows = in_rows.reshape(columns * CORES, -1, 3, group).transpose(1, 2, 0, 3)
    in_rows = in_rows.reshape(-1, 3 * width)
    in_full = lax.all_gather(in_rows, ("z", "c"), axis=0, tiled=True)
    input_rows = grad_middle + norm_back(grad_one, unit_one, rate_one, gain_one)
    input_rows = tie(input_rows, up_rows, down_full)
    input_gradient = from_planes(input_rows.astype(bf16).reshape(planes, -1, width))
    mixed_cores = mixed_owned.reshape(columns, CORES, -1, group)

    def near_rows(core):
        rows = []
        for d in range(columns):
            size = (1, 1) + mixed_cores.shape[2:]
            rows.append(lax.dynamic_slice(mixed_cores, (me_f ^ d, core, 0, 0), size))
        return jnp.concatenate(rows).reshape(-1, group)

    out_term = contract(near_rows(me_c), branch_mine, 0, 0)
    out_term = (out_term + contract(near_rows(1 - me_c), branch_other, 0, 0)).astype(bf16)

    sums = jnp.stack(
        [
            jnp.sum(grad_one * unit_one, axis=0),
            jnp.sum(grad_one, axis=0),
            jnp.sum(grad_branch.astype(f32), axis=0),
            jnp.sum(grad_two * unit_two, axis=0),
            jnp.sum(grad_two, axis=0),
            jnp.sum(grad_rows, axis=0),
        ]
    )
    sums = butterfly(sums, ("c", "f"))
    biases = jnp.concatenate(
        [
            jnp.sum(grad_hidden.astype(f32), axis=0),
            jnp.sum(dq.astype(f32), axis=0),
            jnp.sum(dv.astype(f32), axis=0),
        ]
    )
    biases = jnp.pad(biases, (0, (16 * planes - 6) * width - biases.shape[0])).reshape(-1, width)
    out_term = jnp.concatenate([out_term, sums.astype(bf16), biases.astype(bf16)])
    out_share = exchange(out_term.reshape(planes, -1, width), "z").astype(f32)
    out_share = jnp.sum(out_share, axis=0).astype(bf16)
    out_full = lax.all_gather(out_share, ("z", "c"), axis=0, tiled=False)

    layer_rows = tie(middle + layer_sum + bias_reduce, input_gradient).astype(bf16)
    layer_output = from_planes(layer_rows.reshape(planes, -1, width))
    input_gradient = input_gradient.astype(f32)

    out_full = out_full.reshape(planes, CORES, -1, width).transpose(1, 0, 2, 3)
    first_out, last_out = out_full.reshape(CORES, -1, width).astype(f32) * scaling
    out_gradient = jnp.concatenate([first_out[:group], last_out[:group]])
    sums = pick(first_out[group : group + 6].reshape(6, columns, -1), me_f, 1)
    biases = jnp.stack([rows[group + 6 :].reshape(-1) for rows in (first_out, last_out)])
    up_bias = biases[:, :ff].reshape(CORES, planes, unit).transpose(1, 0, 2).reshape(-1)
    in_bias = biases[:, ff : ff + 2 * group].reshape(CORES, 2, group).transpose(1, 0, 2)
    in_bias = in_bias.reshape(2, -1)
    in_gradient = in_full.astype(f32) * scaling
    down_gradient = down_full.astype(f32) * scaling
    up_gradient = up_full.astype(f32) * scaling

    return (
        layer_output[None],
        input_gradient[None],
        sums[0],
        sums[1],
        in_gradient,
        in_bias,
        out_gradient,
        sums[2],
        sums[3],
        sums[4],
        up_gradient,
        up_bias,
        down_gradient,
        sums[5],
    )


def solution(mesh):
    columns, seq = mesh.devices.shape
    split = Mesh(mesh.devices.reshape(columns, seq // CORES, CORES), ("f", "z", "c"))
    rows = P("f", ("z", "c"), None)
    vector, matrix, paired = P("f"), P("f", None), P(None, "f")
    return jax.shard_map(
        local,
        mesh=split,
        in_specs=(
            rows,
            P("f", None),
            rows,
            vector,
            vector,
            matrix,
            paired,
            matrix,
            vector,
            vector,
            vector,
            matrix,
            vector,
            matrix,
            vector,
        ),
        out_specs=(
            rows,
            rows,
            vector,
            vector,
            matrix,
            paired,
            matrix,
            vector,
            vector,
            vector,
            matrix,
            vector,
            matrix,
            vector,
        ),
        check_vma=False,
    )
```

```python
import functools

import jax
import jax.numpy as jnp
from jax import lax
from jax.experimental import pallas as pl
from jax.experimental.pallas import tpu as pltpu
from jax.sharding import Mesh, PartitionSpec as P

HEADS = 32
HEAD_DIM = 64
BLOCK = 128
DOCS = 4
TILE = 256
CORES = 2
MASKED = -1e30

epsilon = 1e-05
bf16 = jnp.bfloat16
f32 = jnp.float32


def contract(a, b, da, db):
    return lax.dot_general(a, b, (((da,), (db,)), ((), ())), preferred_element_type=f32)


def tile_bias(bias_ref, slope_ref, pair):
    keys = lax.broadcasted_iota(jnp.int32, (TILE, TILE), 0)
    queries = lax.broadcasted_iota(jnp.int32, (TILE, TILE), 1)
    gap = (keys - queries).astype(f32)
    for h in range(2):
        bias_ref[h] = gap * slope_ref[pair * 2 + h]


def head_halves(block):
    lane = lax.broadcasted_iota(jnp.int32, block.shape, 1)
    zero = jnp.zeros_like(block)
    return [jnp.where((lane // HEAD_DIM) == h, block, zero) for h in range(2)]


def forward_kernel(
    first_ref, slope_ref, q_ref, k_ref, v_ref, low_ref, high_ref, out_ref, lse_ref, vt_ref, bias_ref
):
    qi = pl.program_id(0)
    wide = 2 * HEAD_DIM
    pairs = q_ref.shape[1] // wide
    heads = range(2 * pairs)

    @pl.when(qi == 0)
    def _():
        vt_ref[...] = v_ref[...].T
        for pair in range(pairs):
            tile_bias(bias_ref.at[pl.ds(2 * pair, 2)], slope_ref, pair)

    scale = jnp.asarray(HEAD_DIM**-0.5, bf16)
    queries = []
    for pair in range(pairs):
        queries += head_halves(q_ref[:, pl.ds(pair * wide, wide)] * scale)
    low, high = low_ref[...], high_ref[...]
    rows = lax.broadcasted_iota(jnp.int32, (TILE, TILE), 0)

    def scores_of(h, start):
        keys = k_ref[pl.ds(start, TILE), pl.ds(h // 2 * wide, wide)]
        return contract(keys, queries[h], 1, 1)

    def mix(h, start, weights):
        values = vt_ref[pl.ds(h * HEAD_DIM, HEAD_DIM), pl.ds(start, TILE)]
        return contract(values, weights.astype(bf16), 1, 0)

    here = pl.multiple_of(qi * TILE, TILE)
    inside = (rows >= low - here) & (rows < high - here)
    state = []
    for h in heads:
        scores = jnp.where(inside, scores_of(h, here) - jnp.abs(bias_ref[h]), MASKED)
        peak = jnp.max(scores, axis=0, keepdims=True)
        weights = jnp.exp(scores - peak)
        state += [peak, jnp.sum(weights, axis=0, keepdims=True), mix(h, here, weights)]

    def step(t, state):
        start = pl.multiple_of(t * TILE, TILE)
        seen = rows >= low - start
        away = ((t - qi) * TILE).astype(f32)
        fresh = []
        for h in heads:
            peak, total, mixed = state[3 * h : 3 * h + 3]
            scores = jnp.where(seen, scores_of(h, start) + bias_ref[h], MASKED)
            offset = away * slope_ref[h]
            top = jnp.maximum(peak, jnp.max(scores, axis=0, keepdims=True) + offset)
            weights = jnp.exp(scores + (offset - top))
            shrink = jnp.exp(peak - top)
            total = total * shrink + jnp.sum(weights, axis=0, keepdims=True)
            fresh += [top, total, mixed * shrink + mix(h, start, weights)]
        return tuple(fresh)

    state = lax.fori_loop(first_ref[qi], qi, step, tuple(state))
    for pair in range(pairs):
        sides = [state[3 * h + 2] / state[3 * h + 1] for h in (2 * pair, 2 * pair + 1)]
        out_ref[:, pl.ds(pair * wide, wide)] = jnp.concatenate(sides, axis=0).T.astype(bf16)
        sides = [state[3 * h] + jnp.log(state[3 * h + 1]) for h in (2 * pair, 2 * pair + 1)]
        lse_ref[pair] = jnp.concatenate(sides, axis=0)


def backward_kernel(
    first_ref,
    slope_ref,
    q_ref,
    k_ref,
    v_ref,
    out_ref,
    grad_ref,
    lse_ref,
    low_ref,
    high_ref,
    dq_ref,
    dk_ref,
    dv_ref,
    kt_ref,
    bias_ref,
    dk_sum,
    dv_sum,
    dq_sum,
):
    pair, qi = pl.program_id(0), pl.program_id(1)

    @pl.when(qi == 0)
    def _():
        kt_ref[...] = k_ref[...].T
        tile_bias(bias_ref, slope_ref, pair)
        dk_sum[...] = jnp.zeros_like(dk_sum)
        dv_sum[...] = jnp.zeros_like(dv_sum)

    queries = head_halves(q_ref[...] * jnp.asarray(HEAD_DIM**-0.5, bf16))
    grads = head_halves(grad_ref[...])
    low, high = low_ref[...], high_ref[...]
    rows = lax.broadcasted_iota(jnp.int32, (TILE, TILE), 0)
    product = (grad_ref[...].astype(f32) * out_ref[...].astype(f32)).T
    deltas = [
        jnp.sum(product[h * HEAD_DIM : (h + 1) * HEAD_DIM], axis=0, keepdims=True) for h in range(2)
    ]
    lse = [lse_ref[0, pl.ds(h, 1), :] for h in range(2)]
    dq_sum[...] = jnp.zeros_like(dq_sum)

    def tile(start, on_diagonal, offsets):
        keys = k_ref[pl.ds(start, TILE), :]
        values = v_ref[pl.ds(start, TILE), :]
        seen = rows >= low - start
        if on_diagonal:
            seen = seen & (rows < high - start)
        dk, dv = dk_sum[pl.ds(start, TILE), :], dv_sum[pl.ds(start, TILE), :]
        for h in range(2):
            scores = contract(keys, queries[h], 1, 1)
            if on_diagonal:
                scores = scores - jnp.abs(bias_ref[h]) - lse[h]
            else:
                scores = scores + bias_ref[h] + (offsets[h] - lse[h])
            probs = jnp.exp(jnp.where(seen, scores, MASKED))
            pull = contract(values, grads[h], 1, 1)
            grad_scores = (probs * (pull - deltas[h])).astype(bf16)
            dv = dv + contract(probs.astype(bf16), grads[h], 1, 0)
            dk = dk + contract(grad_scores, queries[h], 1, 0)
            keys_t = kt_ref[pl.ds(h * HEAD_DIM, HEAD_DIM), pl.ds(start, TILE)]
            dq_sum[pl.ds(h * HEAD_DIM, HEAD_DIM), :] += contract(keys_t, grad_scores, 1, 0)
        dk_sum[pl.ds(start, TILE), :] = dk
        dv_sum[pl.ds(start, TILE), :] = dv

    tile(pl.multiple_of(qi * TILE, TILE), True, None)

    def step(t, carry):
        away = ((t - qi) * TILE).astype(f32)
        tile(
            pl.multiple_of(t * TILE, TILE),
            False,
            [away * slope_ref[pair * 2 + h] for h in range(2)],
        )
        return carry

    lax.fori_loop(first_ref[qi], qi, step, 0)
    dq_ref[...] = (dq_sum[...] * HEAD_DIM**-0.5).T.astype(bf16)

    @pl.when(qi == pl.num_programs(1) - 1)
    def _():
        dk_ref[...] = dk_sum[...].astype(bf16)
        dv_ref[...] = dv_sum[...].astype(bf16)


def attention_specs(length, pairs):
    wide = 2 * HEAD_DIM

    def tiles(third):
        return pl.BlockSpec((TILE, wide), lambda p, i, *_: (i, third * pairs + p))

    def whole(third):
        return pl.BlockSpec((length, wide), lambda p, i, *_: (0, third * pairs + p))

    limits = pl.BlockSpec((1, TILE), lambda p, i, *_: (0, i))
    lse = pl.BlockSpec((1, 2, TILE), lambda p, i, *_: (p, 0, i))
    return tiles, whole, limits, lse


def attention(stacked, low, high, first, slopes):
    length, pairs = stacked.shape[0], stacked.shape[1] // (6 * HEAD_DIM)
    width = pairs * 2 * HEAD_DIM
    limits = pl.BlockSpec((1, TILE), lambda i, *_: (0, i))
    return pl.pallas_call(
        forward_kernel,
        grid_spec=pltpu.PrefetchScalarGridSpec(
            num_scalar_prefetch=2,
            grid=(length // TILE,),
            in_specs=[
                pl.BlockSpec((TILE, width), lambda i, *_: (i, 0)),
                pl.BlockSpec((length, width), lambda i, *_: (0, 1)),
                pl.BlockSpec((length, width), lambda i, *_: (0, 2)),
                limits,
                limits,
            ],
            out_specs=[
                pl.BlockSpec((TILE, width), lambda i, *_: (i, 0)),
                pl.BlockSpec((pairs, 2, TILE), lambda i, *_: (0, 0, i)),
            ],
            scratch_shapes=[
                pltpu.VMEM((width, length), bf16),
                pltpu.VMEM((2 * pairs, TILE, TILE), f32),
            ],
        ),
        out_shape=[
            jax.ShapeDtypeStruct((length, width), bf16),
            jax.ShapeDtypeStruct((pairs, 2, length), f32),
        ],
        compiler_params=pltpu.CompilerParams(vmem_limit_bytes=32 << 20),
        cost_estimate=pl.CostEstimate(
            flops=30_000_000_000, bytes_accessed=4 << 20, transcendentals=1 << 20
        ),
        name="attention_forward",
    )(first, slopes, stacked, stacked, stacked, low, high)


def attention_back(stacked, mixed, grads, lse_rows, low, high, first, slopes):
    length, pairs = stacked.shape[0], stacked.shape[1] // (6 * HEAD_DIM)
    tiles, whole, limits, lse = attention_specs(length, pairs)
    shape = jax.ShapeDtypeStruct((length, pairs * 2 * HEAD_DIM), bf16)
    return pl.pallas_call(
        backward_kernel,
        grid_spec=pltpu.PrefetchScalarGridSpec(
            num_scalar_prefetch=2,
            grid=(pairs, length // TILE),
            in_specs=[tiles(0), whole(1), whole(2), tiles(0), tiles(0), lse, limits, limits],
            out_specs=[tiles(0), whole(0), whole(0)],
            scratch_shapes=[
                pltpu.VMEM((2 * HEAD_DIM, length), bf16),
                pltpu.VMEM((2, TILE, TILE), f32),
                pltpu.VMEM((length, 2 * HEAD_DIM), f32),
                pltpu.VMEM((length, 2 * HEAD_DIM), f32),
                pltpu.VMEM((2 * HEAD_DIM, TILE), f32),
            ],
        ),
        out_shape=[shape, shape, shape],
        compiler_params=pltpu.CompilerParams(vmem_limit_bytes=32 << 20),
        cost_estimate=pl.CostEstimate(
            flops=30_000_000_000, bytes_accessed=8 << 20, transcendentals=1 << 20
        ),
        name="attention_backward",
    )(first, slopes, stacked, stacked, stacked, mixed, grads, lse_rows, low, high)


def moments(values):
    centre = jnp.mean(values, axis=-1, keepdims=True)
    offset = values - centre
    rate = lax.rsqrt(jnp.mean(offset * offset, axis=-1, keepdims=True) + epsilon)
    return offset * rate, rate


def norm_back(grads, unit, rate, gain):
    scaled = grads * gain
    mean = jnp.mean(scaled, axis=-1, keepdims=True)
    along = jnp.mean(scaled * unit, axis=-1, keepdims=True)
    return rate * (scaled - mean - unit * along)


def dot(a, b):
    return jnp.dot(a, b, preferred_element_type=f32)


def gelu_parts(values):
    phi = 0.5 * (1.0 + lax.erf(values * (0.5**0.5)))
    density = jnp.exp(-0.5 * values * values) * 0.3989422804014327
    return values * phi, phi + values * density


def pick(values, index, axis):
    return lax.dynamic_index_in_dim(values, index, axis, keepdims=False)


def put(values, piece, *index):
    return lax.dynamic_update_slice(values, piece, index)


def send(values, axis, distance):
    n = lax.axis_size(axis)
    return lax.ppermute(values, axis, [(i, i ^ distance) for i in range(n)])


def butterfly(values, axes):
    for axis in axes:
        distance = 1
        while distance < lax.axis_size(axis):
            values = values + send(values, axis, distance)
            distance *= 2
    return values


def tie(values, *others):
    for other in others:
        first = lax.slice(other, (0,) * other.ndim, (1,) * other.ndim).reshape(())
        values = values + (first.astype(f32) * 0.0).astype(values.dtype)
    return values


def exchange(values, axis):
    return lax.all_to_all(values, axis, split_axis=0, concat_axis=0, tiled=True)


def to_planes(rows):
    split = rows.reshape((lax.axis_size("f"), -1) + rows.shape[1:])
    return exchange(exchange(split, "f"), "z")


def from_planes(blocks):
    rows = exchange(exchange(blocks, "z"), "f")
    return rows.reshape((-1,) + blocks.shape[2:])


def by_position(values, blocks):
    split = values.reshape(lax.axis_size("f"), CORES, blocks, -1, values.shape[-1])
    return split.transpose(2, 1, 0, 3, 4).reshape(values.shape)


def by_owner(values, blocks):
    split = values.reshape(blocks, CORES, lax.axis_size("f"), -1, values.shape[-1])
    return split.transpose(2, 1, 0, 3, 4).reshape(values.shape)


def core_gather(own):
    n = lax.axis_size("f")
    half = own.shape[0] // 2
    if n != 4:
        return jnp.concatenate([own] + [send(own, "f", d) for d in range(1, n)])
    along_x, along_y = send(own, "f", 1), send(own, "f", 2)
    far = [send(along_x[:half], "f", 2), send(along_y[half:], "f", 1)]
    return jnp.concatenate([own, along_x, along_y] + far)


def plane_scatter(partial, *floor):
    n = lax.axis_size("f")
    me_f, me_c = lax.axis_index("f"), lax.axis_index("c")
    split = partial.reshape(n, CORES, -1, partial.shape[-1])
    half = split.shape[2] // 2
    other = send(tie(pick(split, 1 - me_c, 1), *floor), "c", 1)
    near = (pick(split, me_c, 1).astype(f32) + other.astype(f32)).astype(bf16)

    def block(distance):
        return pick(near, me_f ^ distance, 0)

    if n == 4:
        far = block(3)
        for_y, for_x = send(far[:half], "f", 1), send(far[half:], "f", 2)
        near_x, near_y = block(1), block(2)
        near_x = jnp.concatenate([near_x[:half], near_x[half:] + for_x])
        near_y = jnp.concatenate([near_y[:half] + for_y, near_y[half:]])
        from_x, from_y = send(near_x, "f", 1), send(near_y, "f", 2)
        return block(0).astype(f32) + from_x.astype(f32) + from_y.astype(f32)
    total = block(0).astype(f32)
    for d in range(1, n):
        total = total + send(block(d), "f", d).astype(f32)
    return total


def heads_to_tokens(mixed):
    devices = lax.axis_size("f") * CORES
    parts = exchange(mixed.reshape(devices, -1, mixed.shape[-1]), ("f", "c"))
    return parts.transpose(1, 0, 2).reshape(parts.shape[1], -1)


def tokens_to_heads(rows):
    devices = lax.axis_size("f") * CORES
    parts = rows.reshape(rows.shape[0], devices, -1).transpose(1, 0, 2)
    return exchange(parts, ("f", "c")).reshape(-1, parts.shape[-1])


def local(
    inputs,
    documents,
    cotangent,
    attend_gain,
    attend_shift,
    project_in,
    project_bias,
    project_out,
    output_bias,
    feed_gain,
    feed_shift,
    expand_weight,
    expand_bias,
    reduce_weight,
    reduce_bias,
):
    columns, planes = lax.axis_size("f"), lax.axis_size("z")
    me_f, me_z, me_c = lax.axis_index("f"), lax.axis_index("z"), lax.axis_index("c")
    width = inputs.shape[2]
    length = documents.shape[1]
    hidden = expand_weight.shape[1]
    device_heads = HEADS // (columns * CORES)
    group = device_heads * HEAD_DIM
    ff = hidden // (columns * CORES)
    unit = ff // planes
    scaling = (columns * length) ** (-0.5)

    vectors = jnp.stack([attend_gain, attend_shift, output_bias, feed_gain, feed_shift, reduce_bias])
    vectors = lax.all_gather(vectors, "f", axis=1, tiled=True).astype(f32)
    gain_one, shift_one, bias_out, gain_two, shift_two, bias_reduce = vectors

    split = tie(inputs[0], vectors).reshape(columns, -1, width)
    split = exchange(split, "f")
    tokens = exchange(split, "z").reshape(-1, width)
    turn = [(a * planes + b, b * planes + a) for a in range(columns) for b in range(planes)]
    docs = lax.ppermute(documents, ("f", "z"), turn)

    deep = project_in.shape[0]
    weight_in = jnp.zeros((width, 3 * group), bf16)
    for d in range(columns):
        column = ((me_f ^ d) * CORES + me_c) * group
        piece = jnp.concatenate(
            [
                lax.dynamic_slice(project_in, (0, third * width + column), (deep, group))
                for third in range(3)
            ],
            axis=1,
        )
        piece = send(piece, "f", d) if d else piece
        weight_in = put(weight_in, piece, (me_f ^ d) * deep, 0)
    grad_own = to_planes(tie(cotangent[0], tokens)).reshape(-1, width)
    strip = expand_weight.shape[0] // planes
    strips = lax.dynamic_slice_in_dim(expand_weight, me_z * strip, strip)
    turned = jnp.stack(
        [
            jnp.concatenate(
                [
                    lax.dynamic_slice(
                        strips, (0, (j * planes + p) * CORES * unit + me_c * unit), (strip, unit)
                    )
                    for p in range(planes)
                ],
                axis=1,
            )
            for j in range(columns)
        ]
    )
    turned = exchange(tie(turned, tokens), "f")
    up_pieces = [send(turned, "z", e) if e else turned for e in range(planes)]
    weight_down = pick(reduce_weight.reshape(planes, CORES, unit, width), me_c, 1).reshape(ff, width)
    bias_pair = pick(project_bias.reshape(2, CORES, group), me_c, 1).astype(f32)
    bias_in = jnp.concatenate([bias_pair[0], jnp.zeros((group,), f32), bias_pair[1]])
    bias_up = pick(expand_bias.reshape(planes, CORES, unit), me_c, 1).reshape(ff).astype(f32)

    doc_row = docs[0]
    position = jnp.arange(length, dtype=jnp.int32)
    low = jnp.zeros_like(doc_row)
    end = jnp.zeros_like(doc_row)
    for d in range(DOCS):
        low = jnp.where(doc_row == d, jnp.sum((doc_row < d).astype(jnp.int32)), low)
        end = jnp.where(doc_row == d, jnp.sum((doc_row <= d).astype(jnp.int32)), end)
    high = jnp.minimum(end, (position // BLOCK + 1) * BLOCK)
    first = low[::TILE] // TILE
    low, high = low[None], high[None]
    first_head = (me_f * CORES + me_c) * device_heads
    heads = first_head + 1 + jnp.arange(device_heads, dtype=jnp.int32)
    slopes = 2.0 ** (-8.0 * heads.astype(f32) / HEADS)

    token_rows = tie(tokens.astype(f32), weight_in)
    unit_one, rate_one = moments(token_rows)
    normed_one = (unit_one * gain_one + shift_one).astype(bf16)
    normed_one = lax.all_gather(normed_one, ("f", "c"), axis=0, tiled=True)
    stacked = tie(dot(normed_one, weight_in) + bias_in, grad_own, turned, low, high)
    stacked = by_position(stacked.astype(bf16), planes)
    mine = tie(pick(project_out.reshape(CORES, -1, width), me_c, 0), grad_own)
    weight_out = lax.all_gather(mine, ("f", "c"), axis=0, tiled=True)
    mixed, lse_rows = attention(stacked, low, high, first, slopes)
    mixed_owned = by_owner(mixed, planes)
    weight_up = jnp.zeros((columns, planes, strip, ff), bf16)
    for e in range(planes):
        piece = up_pieces[e][:, None]
        weight_up = put(weight_up, piece, 0, me_z ^ e, 0, 0)
    weight_up = weight_up.reshape(width, ff)
    middle = token_rows + (dot(heads_to_tokens(mixed_owned), weight_out) + bias_out)
    unit_two, rate_two = moments(middle)
    grad_all = lax.all_gather(tie(grad_own, mixed), ("f", "c"), axis=0, tiled=True)
    normed_two = (unit_two * gain_two + shift_two).astype(bf16)
    normed_two = lax.all_gather(normed_two, ("f", "c"), axis=0, tiled=True)
    hidden_pre = dot(normed_two, weight_up) + bias_up
    active, slope = gelu_parts(hidden_pre)
    active = active.astype(bf16)

    down_term = contract(active, grad_all, 0, 0).astype(bf16)
    grad_active = tie(contract(grad_all, weight_down, 1, 1), down_term)
    grad_hidden = (grad_active * slope).astype(bf16)
    grad_partial = contract(grad_hidden, weight_up, 1, 1).astype(bf16)
    up_term = tie(contract(normed_two, grad_hidden, 0, 0), grad_partial).astype(bf16)
    forward_partial = tie(dot(active, weight_down), up_term).astype(bf16)
    down_share = lax.psum_scatter(down_term, "z", scatter_dimension=0, tiled=True)
    grad_two = tie(plane_scatter(grad_partial), up_term, forward_partial)
    up_share = up_term.reshape(columns, -1, ff)
    up_share = lax.psum_scatter(up_share, "z", scatter_dimension=1, tiled=True)

    grad_rows = grad_own.astype(f32)
    grad_middle = grad_rows + norm_back(grad_two, unit_two, rate_two, gain_two)
    grad_branch = grad_middle.astype(bf16)
    grad_mixed_owned = tokens_to_heads(contract(grad_branch, weight_out, 1, 1).astype(bf16))
    grad_mixed = tie(by_position(grad_mixed_owned, planes), down_share)
    branch_mine = core_gather(tie(grad_branch, grad_mixed_owned))
    branch_other = send(branch_mine, "c", 1)
    layer_sum = plane_scatter(forward_partial, grad_mixed_owned)
    dq, dk, dv = attention_back(stacked, mixed, grad_mixed, lse_rows, low, high, first, slopes)
    grad_projected = by_owner(jnp.concatenate([dq, dk, dv], axis=1), planes)
    grad_partial = contract(grad_projected, weight_in, 1, 1).astype(bf16)
    in_term = tie(contract(normed_one, grad_projected, 0, 0), grad_partial, up_share).astype(bf16)
    down_full = lax.all_gather(down_share, ("z", "c"), axis=0, tiled=True)
    grad_one = tie(plane_scatter(grad_partial), in_term)

    up_rows = tie(up_share, grad_one).reshape(columns * CORES, -1, ff)
    up_rows = exchange(up_rows, ("f", "c")).reshape(columns, CORES, -1, planes, unit)
    up_rows = up_rows.transpose(2, 0, 3, 1, 4).reshape(-1, hidden)
    in_share = in_term.reshape(columns, -1, 3 * group)
    in_share = lax.psum_scatter(in_share, "z", scatter_dimension=1, tiled=True)
    up_full = lax.all_gather(up_rows, ("z", "c"), axis=0, tiled=True)
    in_rows = exchange(in_share.reshape(columns * CORES, -1, 3 * group), ("f", "c"))
    in_rows = in_rows.reshape(columns * CORES, -1, 3, group).transpose(1, 2, 0, 3)
    in_rows = in_rows.reshape(-1, 3 * width)
    in_full = lax.all_gather(in_rows, ("z", "c"), axis=0, tiled=True)
    input_rows = grad_middle + norm_back(grad_one, unit_one, rate_one, gain_one)
    input_rows = tie(input_rows, up_rows, down_full)
    input_gradient = from_planes(input_rows.astype(bf16).reshape(planes, -1, width))
    mixed_cores = mixed_owned.reshape(columns, CORES, -1, group)

    def near_rows(core):
        rows = []
        for d in range(columns):
            size = (1, 1) + mixed_cores.shape[2:]
            rows.append(lax.dynamic_slice(mixed_cores, (me_f ^ d, core, 0, 0), size))
        return jnp.concatenate(rows).reshape(-1, group)

    out_term = contract(near_rows(me_c), branch_mine, 0, 0)
    out_term = (out_term + contract(near_rows(1 - me_c), branch_other, 0, 0)).astype(bf16)

    sums = jnp.stack(
        [
            jnp.sum(grad_one * unit_one, axis=0),
            jnp.sum(grad_one, axis=0),
            jnp.sum(grad_branch.astype(f32), axis=0),
            jnp.sum(grad_two * unit_two, axis=0),
            jnp.sum(grad_two, axis=0),
            jnp.sum(grad_rows, axis=0),
        ]
    )
    sums = butterfly(sums, ("c", "f"))
    biases = jnp.concatenate(
        [
            jnp.sum(grad_hidden.astype(f32), axis=0),
            jnp.sum(dq.astype(f32), axis=0),
            jnp.sum(dv.astype(f32), axis=0),
        ]
    )
    biases = jnp.pad(biases, (0, (16 * planes - 6) * width - biases.shape[0])).reshape(-1, width)
    out_term = jnp.concatenate([out_term, sums.astype(bf16), biases.astype(bf16)])
    out_share = exchange(out_term.reshape(planes, -1, width), "z").astype(f32)
    out_share = jnp.sum(out_share, axis=0).astype(bf16)
    out_full = lax.all_gather(out_share, ("z", "c"), axis=0, tiled=False)

    layer_rows = tie(middle + layer_sum + bias_reduce, input_gradient).astype(bf16)
    layer_output = from_planes(layer_rows.reshape(planes, -1, width))
    input_gradient = input_gradient.astype(f32)

    out_full = out_full.reshape(planes, CORES, -1, width).transpose(1, 0, 2, 3)
    first_out, last_out = out_full.reshape(CORES, -1, width).astype(f32) * scaling
    out_gradient = jnp.concatenate([first_out[:group], last_out[:group]])
    sums = pick(first_out[group : group + 6].reshape(6, columns, -1), me_f, 1)
    biases = jnp.stack([rows[group + 6 :].reshape(-1) for rows in (first_out, last_out)])
    up_bias = biases[:, :ff].reshape(CORES, planes, unit).transpose(1, 0, 2).reshape(-1)
    in_bias = biases[:, ff : ff + 2 * group].reshape(CORES, 2, group).transpose(1, 0, 2)
    in_bias = in_bias.reshape(2, -1)
    in_gradient = in_full.astype(f32) * scaling
    down_gradient = down_full.astype(f32) * scaling
    up_gradient = up_full.astype(f32) * scaling

    return (
        layer_output[None],
        input_gradient[None],
        sums[0],
        sums[1],
        in_gradient,
        in_bias,
        out_gradient,
        sums[2],
        sums[3],
        sums[4],
        up_gradient,
        up_bias,
        down_gradient,
        sums[5],
    )


def solution(mesh):
    columns, seq = mesh.devices.shape
    split = Mesh(mesh.devices.reshape(columns, seq // CORES, CORES), ("f", "z", "c"))
    rows = P("f", ("z", "c"), None)
    vector, matrix, paired = P("f"), P("f", None), P(None, "f")
    return jax.shard_map(
        local,
        mesh=split,
        in_specs=(
            rows,
            P("f", None),
            rows,
            vector,
            vector,
            matrix,
            paired,
            matrix,
            vector,
            vector,
            vector,
            matrix,
            vector,
            matrix,
            vector,
        ),
        out_specs=(
            rows,
            rows,
            vector,
            vector,
            matrix,
            paired,
            matrix,
            vector,
            vector,
            vector,
            matrix,
            vector,
            matrix,
            vector,
        ),
        check_vma=False,
    )
```

```python
import functools

import jax
import jax.numpy as jnp
from jax import lax
from jax.experimental import pallas as pl
from jax.experimental.pallas import tpu as pltpu
from jax.sharding import Mesh, PartitionSpec as P

HEADS = 32
HEAD_DIM = 64
BLOCK = 128
DOCS = 4
TILE = 256
CORES = 2
MASKED = -1e30

epsilon = 1e-05
bf16 = jnp.bfloat16
f32 = jnp.float32


def contract(a, b, da, db):
    return lax.dot_general(a, b, (((da,), (db,)), ((), ())), preferred_element_type=f32)


def tile_bias(bias_ref, slope_ref, pair):
    keys = lax.broadcasted_iota(jnp.int32, (TILE, TILE), 0)
    queries = lax.broadcasted_iota(jnp.int32, (TILE, TILE), 1)
    gap = (keys - queries).astype(f32)
    for h in range(2):
        bias_ref[h] = gap * slope_ref[pair * 2 + h]


def head_halves(block):
    lane = lax.broadcasted_iota(jnp.int32, block.shape, 1)
    zero = jnp.zeros_like(block)
    return [jnp.where((lane // HEAD_DIM) == h, block, zero) for h in range(2)]


def forward_kernel(
    first_ref, slope_ref, q_ref, k_ref, v_ref, low_ref, high_ref, out_ref, lse_ref, vt_ref, bias_ref
):
    qi = pl.program_id(0)
    wide = 2 * HEAD_DIM
    pairs = q_ref.shape[1] // wide
    heads = range(2 * pairs)

    @pl.when(qi == 0)
    def _():
        vt_ref[...] = v_ref[...].T
        for pair in range(pairs):
            tile_bias(bias_ref.at[pl.ds(2 * pair, 2)], slope_ref, pair)

    scale = jnp.asarray(HEAD_DIM**-0.5, bf16)
    queries = []
    for pair in range(pairs):
        queries += head_halves(q_ref[:, pl.ds(pair * wide, wide)] * scale)
    low, high = low_ref[...], high_ref[...]
    rows = lax.broadcasted_iota(jnp.int32, (TILE, TILE), 0)

    def scores_of(h, start):
        keys = k_ref[pl.ds(start, TILE), pl.ds(h // 2 * wide, wide)]
        return contract(keys, queries[h], 1, 1)

    def mix(h, start, weights):
        values = vt_ref[pl.ds(h * HEAD_DIM, HEAD_DIM), pl.ds(start, TILE)]
        return contract(values, weights.astype(bf16), 1, 0)

    here = pl.multiple_of(qi * TILE, TILE)
    inside = (rows >= low - here) & (rows < high - here)
    state = []
    for h in heads:
        scores = jnp.where(inside, scores_of(h, here) - jnp.abs(bias_ref[h]), MASKED)
        peak = jnp.max(scores, axis=0, keepdims=True)
        weights = jnp.exp(scores - peak)
        state += [peak, jnp.sum(weights, axis=0, keepdims=True), mix(h, here, weights)]

    def step(t, state):
        start = pl.multiple_of(t * TILE, TILE)
        seen = rows >= low - start
        away = ((t - qi) * TILE).astype(f32)
        fresh = []
        for h in heads:
            peak, total, mixed = state[3 * h : 3 * h + 3]
            scores = jnp.where(seen, scores_of(h, start) + bias_ref[h], MASKED)
            offset = away * slope_ref[h]
            top = jnp.maximum(peak, jnp.max(scores, axis=0, keepdims=True) + offset)
            weights = jnp.exp(scores + (offset - top))
            shrink = jnp.exp(peak - top)
            total = total * shrink + jnp.sum(weights, axis=0, keepdims=True)
            fresh += [top, total, mixed * shrink + mix(h, start, weights)]
        return tuple(fresh)

    state = lax.fori_loop(first_ref[qi], qi, step, tuple(state))
    for pair in range(pairs):
        sides = [state[3 * h + 2] / state[3 * h + 1] for h in (2 * pair, 2 * pair + 1)]
        out_ref[:, pl.ds(pair * wide, wide)] = jnp.concatenate(sides, axis=0).T.astype(bf16)
        sides = [state[3 * h] + jnp.log(state[3 * h + 1]) for h in (2 * pair, 2 * pair + 1)]
        lse_ref[pair] = jnp.concatenate(sides, axis=0)


def backward_kernel(
    first_ref,
    slope_ref,
    q_ref,
    k_ref,
    v_ref,
    out_ref,
    grad_ref,
    lse_ref,
    low_ref,
    high_ref,
    dq_ref,
    dk_ref,
    dv_ref,
    kt_ref,
    bias_ref,
    dk_sum,
    dv_sum,
    dq_sum,
):
    pair, qi = pl.program_id(0), pl.program_id(1)

    @pl.when(qi == 0)
    def _():
        kt_ref[...] = k_ref[...].T
        tile_bias(bias_ref, slope_ref, pair)
        dk_sum[...] = jnp.zeros_like(dk_sum)
        dv_sum[...] = jnp.zeros_like(dv_sum)

    queries = head_halves(q_ref[...] * jnp.asarray(HEAD_DIM**-0.5, bf16))
    grads = head_halves(grad_ref[...])
    low, high = low_ref[...], high_ref[...]
    rows = lax.broadcasted_iota(jnp.int32, (TILE, TILE), 0)
    product = (grad_ref[...].astype(f32) * out_ref[...].astype(f32)).T
    deltas = [
        jnp.sum(product[h * HEAD_DIM : (h + 1) * HEAD_DIM], axis=0, keepdims=True) for h in range(2)
    ]
    lse = [lse_ref[0, pl.ds(h, 1), :] for h in range(2)]
    dq_sum[...] = jnp.zeros_like(dq_sum)

    def tile(start, on_diagonal, offsets):
        keys = k_ref[pl.ds(start, TILE), :]
        values = v_ref[pl.ds(start, TILE), :]
        seen = rows >= low - start
        if on_diagonal:
            seen = seen & (rows < high - start)
        dk, dv = dk_sum[pl.ds(start, TILE), :], dv_sum[pl.ds(start, TILE), :]
        for h in range(2):
            scores = contract(keys, queries[h], 1, 1)
            if on_diagonal:
                scores = scores - jnp.abs(bias_ref[h]) - lse[h]
            else:
                scores = scores + bias_ref[h] + (offsets[h] - lse[h])
            probs = jnp.exp(jnp.where(seen, scores, MASKED))
            pull = contract(values, grads[h], 1, 1)
            grad_scores = (probs * (pull - deltas[h])).astype(bf16)
            dv = dv + contract(probs.astype(bf16), grads[h], 1, 0)
            dk = dk + contract(grad_scores, queries[h], 1, 0)
            keys_t = kt_ref[pl.ds(h * HEAD_DIM, HEAD_DIM), pl.ds(start, TILE)]
            dq_sum[pl.ds(h * HEAD_DIM, HEAD_DIM), :] += contract(keys_t, grad_scores, 1, 0)
        dk_sum[pl.ds(start, TILE), :] = dk
        dv_sum[pl.ds(start, TILE), :] = dv

    tile(pl.multiple_of(qi * TILE, TILE), True, None)

    def step(t, carry):
        away = ((t - qi) * TILE).astype(f32)
        tile(
            pl.multiple_of(t * TILE, TILE),
            False,
            [away * slope_ref[pair * 2 + h] for h in range(2)],
        )
        return carry

    lax.fori_loop(first_ref[qi], qi, step, 0)
    dq_ref[...] = (dq_sum[...] * HEAD_DIM**-0.5).T.astype(bf16)

    @pl.when(qi == pl.num_programs(1) - 1)
    def _():
        dk_ref[...] = dk_sum[...].astype(bf16)
        dv_ref[...] = dv_sum[...].astype(bf16)


def attention_specs(length, pairs):
    wide = 2 * HEAD_DIM

    def tiles(third):
        return pl.BlockSpec((TILE, wide), lambda p, i, *_: (i, third * pairs + p))

    def whole(third):
        return pl.BlockSpec((length, wide), lambda p, i, *_: (0, third * pairs + p))

    limits = pl.BlockSpec((1, TILE), lambda p, i, *_: (0, i))
    lse = pl.BlockSpec((1, 2, TILE), lambda p, i, *_: (p, 0, i))
    return tiles, whole, limits, lse


def attention(stacked, low, high, first, slopes):
    length, pairs = stacked.shape[0], stacked.shape[1] // (6 * HEAD_DIM)
    width = pairs * 2 * HEAD_DIM
    limits = pl.BlockSpec((1, TILE), lambda i, *_: (0, i))
    return pl.pallas_call(
        forward_kernel,
        grid_spec=pltpu.PrefetchScalarGridSpec(
            num_scalar_prefetch=2,
            grid=(length // TILE,),
            in_specs=[
                pl.BlockSpec((TILE, width), lambda i, *_: (i, 0)),
                pl.BlockSpec((length, width), lambda i, *_: (0, 1)),
                pl.BlockSpec((length, width), lambda i, *_: (0, 2)),
                limits,
                limits,
            ],
            out_specs=[
                pl.BlockSpec((TILE, width), lambda i, *_: (i, 0)),
                pl.BlockSpec((pairs, 2, TILE), lambda i, *_: (0, 0, i)),
            ],
            scratch_shapes=[
                pltpu.VMEM((width, length), bf16),
                pltpu.VMEM((2 * pairs, TILE, TILE), f32),
            ],
        ),
        out_shape=[
            jax.ShapeDtypeStruct((length, width), bf16),
            jax.ShapeDtypeStruct((pairs, 2, length), f32),
        ],
        compiler_params=pltpu.CompilerParams(vmem_limit_bytes=32 << 20),
        cost_estimate=pl.CostEstimate(
            flops=30_000_000_000, bytes_accessed=4 << 20, transcendentals=1 << 20
        ),
        name="attention_forward",
    )(first, slopes, stacked, stacked, stacked, low, high)


def attention_back(stacked, mixed, grads, lse_rows, low, high, first, slopes):
    length, pairs = stacked.shape[0], stacked.shape[1] // (6 * HEAD_DIM)
    tiles, whole, limits, lse = attention_specs(length, pairs)
    shape = jax.ShapeDtypeStruct((length, pairs * 2 * HEAD_DIM), bf16)
    return pl.pallas_call(
        backward_kernel,
        grid_spec=pltpu.PrefetchScalarGridSpec(
            num_scalar_prefetch=2,
            grid=(pairs, length // TILE),
            in_specs=[tiles(0), whole(1), whole(2), tiles(0), tiles(0), lse, limits, limits],
            out_specs=[tiles(0), whole(0), whole(0)],
            scratch_shapes=[
                pltpu.VMEM((2 * HEAD_DIM, length), bf16),
                pltpu.VMEM((2, TILE, TILE), f32),
                pltpu.VMEM((length, 2 * HEAD_DIM), f32),
                pltpu.VMEM((length, 2 * HEAD_DIM), f32),
                pltpu.VMEM((2 * HEAD_DIM, TILE), f32),
            ],
        ),
        out_shape=[shape, shape, shape],
        compiler_params=pltpu.CompilerParams(vmem_limit_bytes=32 << 20),
        cost_estimate=pl.CostEstimate(
            flops=30_000_000_000, bytes_accessed=8 << 20, transcendentals=1 << 20
        ),
        name="attention_backward",
    )(first, slopes, stacked, stacked, stacked, mixed, grads, lse_rows, low, high)


def moments(values):
    centre = jnp.mean(values, axis=-1, keepdims=True)
    offset = values - centre
    rate = lax.rsqrt(jnp.mean(offset * offset, axis=-1, keepdims=True) + epsilon)
    return offset * rate, rate


def norm_back(grads, unit, rate, gain):
    scaled = grads * gain
    mean = jnp.mean(scaled, axis=-1, keepdims=True)
    along = jnp.mean(scaled * unit, axis=-1, keepdims=True)
    return rate * (scaled - mean - unit * along)


def dot(a, b):
    return jnp.dot(a, b, preferred_element_type=f32)


def gelu_parts(values):
    phi = 0.5 * (1.0 + lax.erf(values * (0.5**0.5)))
    density = jnp.exp(-0.5 * values * values) * 0.3989422804014327
    return values * phi, phi + values * density


def pick(values, index, axis):
    return lax.dynamic_index_in_dim(values, index, axis, keepdims=False)


def put(values, piece, *index):
    return lax.dynamic_update_slice(values, piece, index)


def send(values, axis, distance):
    n = lax.axis_size(axis)
    return lax.ppermute(values, axis, [(i, i ^ distance) for i in range(n)])


def butterfly(values, axes):
    for axis in axes:
        distance = 1
        while distance < lax.axis_size(axis):
            values = values + send(values, axis, distance)
            distance *= 2
    return values


def tie(values, *others):
    for other in others:
        first = lax.slice(other, (0,) * other.ndim, (1,) * other.ndim).reshape(())
        values = values + (first.astype(f32) * 0.0).astype(values.dtype)
    return values


def exchange(values, axis):
    return lax.all_to_all(values, axis, split_axis=0, concat_axis=0, tiled=True)


def to_planes(rows):
    split = rows.reshape((lax.axis_size("f"), -1) + rows.shape[1:])
    return exchange(exchange(split, "f"), "z")


def from_planes(blocks):
    rows = exchange(exchange(blocks, "z"), "f")
    return rows.reshape((-1,) + blocks.shape[2:])


def by_position(values, blocks):
    split = values.reshape(lax.axis_size("f"), CORES, blocks, -1, values.shape[-1])
    return split.transpose(2, 1, 0, 3, 4).reshape(values.shape)


def by_owner(values, blocks):
    split = values.reshape(blocks, CORES, lax.axis_size("f"), -1, values.shape[-1])
    return split.transpose(2, 1, 0, 3, 4).reshape(values.shape)


def core_gather(own):
    n = lax.axis_size("f")
    half = own.shape[0] // 2
    if n != 4:
        return jnp.concatenate([own] + [send(own, "f", d) for d in range(1, n)])
    along_x, along_y = send(own, "f", 1), send(own, "f", 2)
    far = [send(along_x[:half], "f", 2), send(along_y[half:], "f", 1)]
    return jnp.concatenate([own, along_x, along_y] + far)


def plane_scatter(partial, *floor):
    n = lax.axis_size("f")
    me_f, me_c = lax.axis_index("f"), lax.axis_index("c")
    split = partial.reshape(n, CORES, -1, partial.shape[-1])
    half = split.shape[2] // 2
    other = send(tie(pick(split, 1 - me_c, 1), *floor), "c", 1)
    near = (pick(split, me_c, 1).astype(f32) + other.astype(f32)).astype(bf16)

    def block(distance):
        return pick(near, me_f ^ distance, 0)

    if n == 4:
        far = block(3)
        for_y, for_x = send(far[:half], "f", 1), send(far[half:], "f", 2)
        near_x, near_y = block(1), block(2)
        near_x = jnp.concatenate([near_x[:half], near_x[half:] + for_x])
        near_y = jnp.concatenate([near_y[:half] + for_y, near_y[half:]])
        from_x, from_y = send(near_x, "f", 1), send(near_y, "f", 2)
        return block(0).astype(f32) + from_x.astype(f32) + from_y.astype(f32)
    total = block(0).astype(f32)
    for d in range(1, n):
        total = total + send(block(d), "f", d).astype(f32)
    return total


def heads_to_tokens(mixed):
    devices = lax.axis_size("f") * CORES
    parts = exchange(mixed.reshape(devices, -1, mixed.shape[-1]), ("f", "c"))
    return parts.transpose(1, 0, 2).reshape(parts.shape[1], -1)


def tokens_to_heads(rows):
    devices = lax.axis_size("f") * CORES
    parts = rows.reshape(rows.shape[0], devices, -1).transpose(1, 0, 2)
    return exchange(parts, ("f", "c")).reshape(-1, parts.shape[-1])


def local(
    inputs,
    documents,
    cotangent,
    attend_gain,
    attend_shift,
    project_in,
    project_bias,
    project_out,
    output_bias,
    feed_gain,
    feed_shift,
    expand_weight,
    expand_bias,
    reduce_weight,
    reduce_bias,
):
    columns, planes = lax.axis_size("f"), lax.axis_size("z")
    me_f, me_z, me_c = lax.axis_index("f"), lax.axis_index("z"), lax.axis_index("c")
    width = inputs.shape[2]
    length = documents.shape[1]
    hidden = expand_weight.shape[1]
    device_heads = HEADS // (columns * CORES)
    group = device_heads * HEAD_DIM
    ff = hidden // (columns * CORES)
    unit = ff // planes
    scaling = (columns * length) ** (-0.5)

    vectors = jnp.stack([attend_gain, attend_shift, output_bias, feed_gain, feed_shift, reduce_bias])
    vectors = lax.all_gather(vectors, "f", axis=1, tiled=True).astype(f32)
    gain_one, shift_one, bias_out, gain_two, shift_two, bias_reduce = vectors

    split = tie(inputs[0], vectors).reshape(columns, -1, width)
    split = exchange(split, "f")
    tokens = exchange(split, "z").reshape(-1, width)
    turn = [(a * planes + b, b * planes + a) for a in range(columns) for b in range(planes)]
    docs = lax.ppermute(documents, ("f", "z"), turn)

    deep = project_in.shape[0]
    weight_in = jnp.zeros((width, 3 * group), bf16)
    in_pieces = []
    for d in range(columns):
        column = ((me_f ^ d) * CORES + me_c) * group
        piece = jnp.concatenate(
            [
                lax.dynamic_slice(project_in, (0, third * width + column), (deep, group))
                for third in range(3)
            ],
            axis=1,
        )
        piece = send(piece, "f", d) if d else piece
        in_pieces.append(piece)
        weight_in = put(weight_in, piece, (me_f ^ d) * deep, 0)
    grad_own = to_planes(tie(cotangent[0], tokens)).reshape(-1, width)
    strip = expand_weight.shape[0] // planes
    strips = lax.dynamic_slice_in_dim(expand_weight, me_z * strip, strip)
    turned = jnp.stack(
        [
            jnp.concatenate(
                [
                    lax.dynamic_slice(
                        strips, (0, (j * planes + p) * CORES * unit + me_c * unit), (strip, unit)
                    )
                    for p in range(planes)
                ],
                axis=1,
            )
            for j in range(columns)
        ]
    )
    turned = exchange(tie(turned, tokens), "f")
    up_pieces = [send(turned, "z", e) if e else turned for e in range(planes)]
    weight_down = pick(reduce_weight.reshape(planes, CORES, unit, width), me_c, 1).reshape(ff, width)
    bias_pair = pick(project_bias.reshape(2, CORES, group), me_c, 1).astype(f32)
    bias_in = jnp.concatenate([bias_pair[0], jnp.zeros((group,), f32), bias_pair[1]])
    bias_up = pick(expand_bias.reshape(planes, CORES, unit), me_c, 1).reshape(ff).astype(f32)

    doc_row = docs[0]
    position = jnp.arange(length, dtype=jnp.int32)
    low = jnp.zeros_like(doc_row)
    end = jnp.zeros_like(doc_row)
    for d in range(DOCS):
        low = jnp.where(doc_row == d, jnp.sum((doc_row < d).astype(jnp.int32)), low)
        end = jnp.where(doc_row == d, jnp.sum((doc_row <= d).astype(jnp.int32)), end)
    high = jnp.minimum(end, (position // BLOCK + 1) * BLOCK)
    first = low[::TILE] // TILE
    low, high = low[None], high[None]
    first_head = (me_f * CORES + me_c) * device_heads
    heads = first_head + 1 + jnp.arange(device_heads, dtype=jnp.int32)
    slopes = 2.0 ** (-8.0 * heads.astype(f32) / HEADS)

    token_rows = tie(tokens.astype(f32), *in_pieces[1:])
    unit_one, rate_one = moments(token_rows)
    normed_one = (unit_one * gain_one + shift_one).astype(bf16)
    normed_one = lax.all_gather(normed_one, ("f", "c"), axis=0, tiled=True)
    stacked = tie(dot(normed_one, weight_in) + bias_in, grad_own, turned, low, high)
    stacked = by_position(stacked.astype(bf16), planes)
    mine = tie(pick(project_out.reshape(CORES, -1, width), me_c, 0), grad_own)
    weight_out = lax.all_gather(mine, ("f", "c"), axis=0, tiled=True)
    mixed, lse_rows = attention(stacked, low, high, first, slopes)
    mixed_owned = by_owner(mixed, planes)
    weight_up = jnp.zeros((columns, planes, strip, ff), bf16)
    for e in range(planes):
        piece = up_pieces[e][:, None]
        weight_up = put(weight_up, piece, 0, me_z ^ e, 0, 0)
    weight_up = weight_up.reshape(width, ff)
    middle = token_rows + (dot(heads_to_tokens(mixed_owned), weight_out) + bias_out)
    unit_two, rate_two = moments(middle)
    grad_all = lax.all_gather(tie(grad_own, mixed), ("f", "c"), axis=0, tiled=True)
    normed_two = (unit_two * gain_two + shift_two).astype(bf16)
    normed_two = lax.all_gather(normed_two, ("f", "c"), axis=0, tiled=True)
    hidden_pre = dot(normed_two, weight_up) + bias_up
    active, slope = gelu_parts(hidden_pre)
    active = active.astype(bf16)

    down_term = contract(active, grad_all, 0, 0).astype(bf16)
    grad_active = tie(contract(grad_all, weight_down, 1, 1), down_term)
    grad_hidden = (grad_active * slope).astype(bf16)
    grad_partial = contract(grad_hidden, weight_up, 1, 1).astype(bf16)
    up_term = tie(contract(normed_two, grad_hidden, 0, 0), grad_partial).astype(bf16)
    forward_partial = tie(dot(active, weight_down), up_term).astype(bf16)
    down_share = lax.psum_scatter(down_term, "z", scatter_dimension=0, tiled=True)
    grad_two = tie(plane_scatter(grad_partial), up_term, forward_partial)
    up_share = up_term.reshape(columns, -1, ff)
    up_share = lax.psum_scatter(up_share, "z", scatter_dimension=1, tiled=True)

    grad_rows = grad_own.astype(f32)
    grad_middle = grad_rows + norm_back(grad_two, unit_two, rate_two, gain_two)
    grad_branch = grad_middle.astype(bf16)
    grad_mixed_owned = tokens_to_heads(contract(grad_branch, weight_out, 1, 1).astype(bf16))
    grad_mixed = tie(by_position(grad_mixed_owned, planes), down_share)
    branch_mine = core_gather(tie(grad_branch, grad_mixed_owned))
    branch_other = send(branch_mine, "c", 1)
    layer_sum = plane_scatter(forward_partial, grad_mixed_owned)
    dq, dk, dv = attention_back(stacked, mixed, grad_mixed, lse_rows, low, high, first, slopes)
    grad_projected = by_owner(jnp.concatenate([dq, dk, dv], axis=1), planes)
    grad_partial = contract(grad_projected, weight_in, 1, 1).astype(bf16)
    in_term = tie(contract(normed_one, grad_projected, 0, 0), grad_partial, up_share).astype(bf16)
    down_full = lax.all_gather(down_share, ("z", "c"), axis=0, tiled=True)
    grad_one = tie(plane_scatter(grad_partial), in_term)

    up_rows = tie(up_share, grad_one).reshape(columns * CORES, -1, ff)
    up_rows = exchange(up_rows, ("f", "c")).reshape(columns, CORES, -1, planes, unit)
    up_rows = up_rows.transpose(2, 0, 3, 1, 4).reshape(-1, hidden)
    in_share = in_term.reshape(columns, -1, 3 * group)
    in_share = lax.psum_scatter(in_share, "z", scatter_dimension=1, tiled=True)
    up_full = lax.all_gather(up_rows, ("z", "c"), axis=0, tiled=True)
    in_rows = exchange(in_share.reshape(columns * CORES, -1, 3 * group), ("f", "c"))
    in_rows = in_rows.reshape(columns * CORES, -1, 3, group).transpose(1, 2, 0, 3)
    in_rows = in_rows.reshape(-1, 3 * width)
    in_full = lax.all_gather(in_rows, ("z", "c"), axis=0, tiled=True)
    input_rows = grad_middle + norm_back(grad_one, unit_one, rate_one, gain_one)
    input_rows = tie(input_rows, up_rows, down_full)
    input_gradient = from_planes(input_rows.astype(bf16).reshape(planes, -1, width))
    mixed_cores = mixed_owned.reshape(columns, CORES, -1, group)

    def near_rows(core):
        rows = []
        for d in range(columns):
            size = (1, 1) + mixed_cores.shape[2:]
            rows.append(lax.dynamic_slice(mixed_cores, (me_f ^ d, core, 0, 0), size))
        return jnp.concatenate(rows).reshape(-1, group)

    out_term = contract(near_rows(me_c), branch_mine, 0, 0)
    out_term = (out_term + contract(near_rows(1 - me_c), branch_other, 0, 0)).astype(bf16)

    sums = jnp.stack(
        [
            jnp.sum(grad_one * unit_one, axis=0),
            jnp.sum(grad_one, axis=0),
            jnp.sum(grad_branch.astype(f32), axis=0),
            jnp.sum(grad_two * unit_two, axis=0),
            jnp.sum(grad_two, axis=0),
            jnp.sum(grad_rows, axis=0),
        ]
    )
    sums = butterfly(sums, ("c", "f"))
    biases = jnp.concatenate(
        [
            jnp.sum(grad_hidden.astype(f32), axis=0),
            jnp.sum(dq.astype(f32), axis=0),
            jnp.sum(dv.astype(f32), axis=0),
        ]
    )
    biases = jnp.pad(biases, (0, (8 * planes - 6) * width - biases.shape[0])).reshape(-1, width)
    out_term = jnp.concatenate([out_term, sums.astype(bf16), biases.astype(bf16)])
    out_share = exchange(out_term.reshape(planes, -1, width), "z").astype(f32)
    out_share = jnp.sum(out_share, axis=0).astype(bf16)
    out_full = lax.all_gather(out_share, ("z", "c"), axis=0, tiled=False)

    layer_rows = tie(middle + layer_sum + bias_reduce, input_gradient).astype(bf16)
    layer_output = from_planes(layer_rows.reshape(planes, -1, width))
    input_gradient = input_gradient.astype(f32)

    out_full = out_full.reshape(planes, CORES, -1, width).transpose(1, 0, 2, 3)
    first_out, last_out = out_full.reshape(CORES, -1, width).astype(f32) * scaling
    out_gradient = jnp.concatenate([first_out[:group], last_out[:group]])
    sums = pick(first_out[group : group + 6].reshape(6, columns, -1), me_f, 1)
    biases = jnp.stack([rows[group + 6 :].reshape(-1) for rows in (first_out, last_out)])
    up_bias = biases[:, :ff].reshape(CORES, planes, unit).transpose(1, 0, 2).reshape(-1)
    in_bias = biases[:, ff : ff + 2 * group].reshape(CORES, 2, group).transpose(1, 0, 2)
    in_bias = in_bias.reshape(2, -1)
    in_gradient = in_full.astype(f32) * scaling
    down_gradient = down_full.astype(f32) * scaling
    up_gradient = up_full.astype(f32) * scaling

    return (
        layer_output[None],
        input_gradient[None],
        sums[0],
        sums[1],
        in_gradient,
        in_bias,
        out_gradient,
        sums[2],
        sums[3],
        sums[4],
        up_gradient,
        up_bias,
        down_gradient,
        sums[5],
    )


def solution(mesh):
    columns, seq = mesh.devices.shape
    split = Mesh(mesh.devices.reshape(columns, seq // CORES, CORES), ("f", "z", "c"))
    rows = P("f", ("z", "c"), None)
    vector, matrix, paired = P("f"), P("f", None), P(None, "f")
    return jax.shard_map(
        local,
        mesh=split,
        in_specs=(
            rows,
            P("f", None),
            rows,
            vector,
            vector,
            matrix,
            paired,
            matrix,
            vector,
            vector,
            vector,
            matrix,
            vector,
            matrix,
            vector,
        ),
        out_specs=(
            rows,
            rows,
            vector,
            vector,
            matrix,
            paired,
            matrix,
            vector,
            vector,
            vector,
            matrix,
            vector,
            matrix,
            vector,
        ),
        check_vma=False,
    )
```
